512 devices in a mesh: vox: 64 (over z, x, core), ch: 8 (over y).
Axes of the slice: x: 4, y: 8, z: 8, core: 2. Of those that a mesh axis runs over, the one named last changes fastest.
Arguments:
- features: bfloat16 [128, 262144], P('ch', 'vox'), may hold values from -6 to 6
- conv_weight: bfloat16 [27, 128, 128], P(None, None, 'ch'), may hold values from -0.109375 to 0.109375
- qkv_weight: bfloat16 [3, 128, 128], P(None, None, 'ch')
- out_weight: bfloat16 [128, 128], P('ch'), may hold values from -0.5 to 0.5
- cotangent: bfloat16 [128, 65536], P('ch', 'vox'), may hold values from -6 to 6
- neighbours: int32 [27, 262144], P(None, 'vox'), may hold values from -1 to 4607, as said below
- send_slot: int32 [262144], P('vox'), may hold values from -1 to 1023, as said below
- recv_slot: int32 [65536], P('vox'), may hold values from -1 to 1023, as said below
Outputs:
- block_out: bfloat16 [128, 65536], P('ch', 'vox')
- grad_features: float32 [128, 262144], P('ch', 'vox')
- grad_conv: float32 [27, 128, 128], P(None, None, 'ch')
- grad_qkv: float32 [3, 128, 128], P(None, None, 'ch')
- grad_out: float32 [128, 128], P('ch')
The draws below stay inside these ranges and needn't reach their ends.
Inputs may be any that keep to these rules, and one draw needn't show every extreme that they name: Cell g = d * 4096 + x * 16 * 16 + y * 16 + z sits at grid point (d * 16 + x, y, z) of a grid of 16 * 64 by 16 by 16 points. neighbours[k, g], k = 9 (dx + 1) + 3 (dy + 1) + (dz + 1), is -1 unless both cells are occupied and the point at offset (dx, dy, dz) is in the grid; else it is (x + dx + 1) * 16 * 16 + (y + dy) * 16 + (z + dz), that cell's index in device d's cells extended by 256 cells on each side. A cell is occupied exactly when its send_slot is not -1; the relation is symmetric between offsets k and 26 - k. `send_slot`: an occupied cell of device s holds d * 16 + j: it is row j of the rows that device s sends to the patch of device d. On each device every value appears at most once and the rows to one patch take slots 0 upward. Every device fills all 16 slots of some patch, and some patch receives 16 rows from every device. `recv_slot`: slot i of device d holds s * 16 + j for row j that device s sends to d, or -1 for an empty slot; every row sent to d appears exactly once.
All inputs are finite; a program needn't handle non-finite values.
Results may differ from the reference program's by a relative error of at most 0.028.
The reference program's roundings to bfloat16 on the way count: a program that leaves them out, or rounds other values in their place, can miss the bound.
Values may be sent and summed in bfloat16 or wider, within the bound.
A program may use at most 64 MiB of HBM per device.

```python
import jax
import jax.numpy as jnp
from jax import lax

C = 128
HEADS = 8
PATCH = 1024
BX = 16
FY = 16
FZ = 16
CELLS_DEV = 4096
NCELL = 262144
NH = 65536
CAP = 16
N_VOX = 64


def layout(key):
    slot_cap = PATCH // N_VOX
    cell_count = BX * FY * FZ
    subkeys = jax.random.split(jax.random.fold_in(key, 11), 5)
    shortfall = jax.random.randint(subkeys[0], (N_VOX, N_VOX), 0, slot_cap // 2 + 1)
    busiest = jax.random.randint(subkeys[1], (), 0, N_VOX)
    own_full = jax.random.randint(subkeys[2], (N_VOX,), 0, N_VOX)
    dest_ids = jnp.arange(N_VOX, dtype=jnp.int32)
    shortfall = jnp.where(dest_ids[None, :] == busiest, 0, shortfall)
    shortfall = jnp.where(dest_ids[None, :] == own_full[:, None], 0, shortfall)
    counts = (slot_cap - shortfall).astype(jnp.int32)
    finish_at = jnp.cumsum(counts, axis=1).astype(jnp.int32)
    rank_list = jnp.arange(cell_count, dtype=jnp.int32)
    target = jax.vmap(lambda limits: jnp.searchsorted(limits, rank_list, side='right'))(finish_at).astype(jnp.int32)
    starts = finish_at - counts
    inside = rank_list[None, :] - jnp.take_along_axis(starts, jnp.minimum(target, N_VOX - 1), axis=1)
    slot_rank = jnp.where(target < N_VOX, target * slot_cap + inside, -1).astype(jnp.int32)
    orders = jax.vmap(lambda subkey: jax.random.permutation(subkey, cell_count))(jax.random.split(subkeys[3], N_VOX)).astype(jnp.int32)
    send_table = jnp.zeros((N_VOX, cell_count), jnp.int32).at[jnp.arange(N_VOX, dtype=jnp.int32)[:, None], orders].set(slot_rank)
    arrivals = jax.vmap(lambda subkey: jax.random.permutation(subkey, PATCH))(jax.random.split(subkeys[4], N_VOX)).astype(jnp.int32)
    arrived_count = jnp.take_along_axis(counts.T, arrivals // slot_cap, axis=1)
    recv_table = jnp.where(arrivals % slot_cap < arrived_count, arrivals, -1).astype(jnp.int32)
    grid_x = N_VOX * BX
    occupied = (send_table >= 0).reshape(grid_x, FY, FZ)
    index_grid = jnp.arange(N_VOX * cell_count, dtype=jnp.int32).reshape(grid_x, FY, FZ)
    own_base = index_grid // cell_count * cell_count - FY * FZ
    occupied_pad = jnp.pad(occupied, 1)
    index_pad = jnp.pad(index_grid, 1, constant_values=-1)
    neighbour_lists = []
    for offset_x in (-1, 0, 1):
        for offset_y in (-1, 0, 1):
            for offset_z in (-1, 0, 1):
                shifted_occ = occupied_pad[1 + offset_x:1 + offset_x + grid_x, 1 + offset_y:1 + offset_y + FY, 1 + offset_z:1 + offset_z + FZ]
                shifted_idx = index_pad[1 + offset_x:1 + offset_x + grid_x, 1 + offset_y:1 + offset_y + FY, 1 + offset_z:1 + offset_z + FZ]
                local_idx = shifted_idx - own_base
                neighbour_lists.append(jnp.where(occupied & shifted_occ, local_idx, -1).reshape(-1))
    return (jnp.stack(neighbour_lists).astype(jnp.int32), send_table.reshape(-1), recv_table.reshape(-1))


def draw_neighbours(key, part):
    return layout(key)[0]


def draw_send_slot(key, part):
    return layout(key)[1]


def draw_recv_slot(key, part):
    return layout(key)[2]


def draw_qkv_weight(key, part):
    return (jax.random.normal(key, (3, C, C), jnp.float32) * C ** (-0.5)).astype(jnp.bfloat16)


def block_scale(own_key, shape, cuts, least, high):
    def one(dim, blocks):
        heights = jax.random.uniform(jax.random.fold_in(jax.random.fold_in(own_key, 6), dim), (blocks,), jnp.float32, least / len(cuts), high / len(cuts))
        return jnp.repeat(jnp.exp(heights), shape[dim] // blocks).reshape((-1,) + (1,) * (len(shape) - dim - 1))

    factor_of = one(*cuts[0])
    for cut in cuts[1:]:
        factor_of = factor_of * one(*cut)
    return factor_of


def scatter_about(key, extent, width, reach, cuts=(), kind=jnp.bfloat16):
    entries = width * jax.random.normal(key, extent, jnp.float32)
    if cuts:
        entries = entries * block_scale(key, extent, cuts, -0.22, 0.18)
    return jnp.clip(entries, -reach, reach).astype(kind)


def setup_inputs(seed: int = 0) -> dict:
    key_list = jax.random.split(jax.random.key(seed), 9)
    return {
        "features": scatter_about(key_list[0], (C, NCELL), 1.0, 6.0, ((0, 8), (1, 64))),
        "conv_weight": scatter_about(key_list[1], (27, C, C), (27 * C) ** -0.5, 0.109375, ((2, 8),)),
        "qkv_weight": draw_qkv_weight(jax.random.fold_in(key_list[8], 71), 0),
        "out_weight": scatter_about(key_list[3], (C, C), C ** -0.5, 0.5, ((0, 8),)),
        "cotangent": scatter_about(key_list[4], (C, NH), 1.0, 6.0, ((0, 8), (1, 64))),
        "neighbours": draw_neighbours(jax.random.fold_in(key_list[8], 71), 0),
        "send_slot": draw_send_slot(jax.random.fold_in(key_list[8], 71), 0),
        "recv_slot": draw_recv_slot(jax.random.fold_in(key_list[8], 71), 0),
    }


def attend(query_rows, key_rows, value_rows, live_mask, grad_attn):
    scale = (C // HEADS) ** (-0.5)
    logits = jnp.einsum('hdq,hdk->hqk', query_rows.astype(jnp.float32), key_rows.astype(jnp.float32)) * scale
    logits = jnp.where(live_mask[None, None, :], logits, -1e+30)
    largest = lax.optimization_barrier(jnp.max(logits, axis=-1, keepdims=True))
    exponents = jnp.exp(logits - largest)
    probs = (exponents / lax.optimization_barrier(jnp.sum(exponents, axis=-1, keepdims=True))).astype(jnp.bfloat16)
    probs_f32 = probs.astype(jnp.float32)
    attended = jnp.einsum('hqk,hdk->hdq', probs_f32, value_rows.astype(jnp.float32)).astype(jnp.bfloat16)
    grad_logits = jnp.einsum('hdq,hdk->hqk', grad_attn.astype(jnp.float32), value_rows.astype(jnp.float32))
    grad_scores = (probs_f32 * (grad_logits - lax.optimization_barrier(jnp.sum(probs_f32 * grad_logits, axis=-1, keepdims=True))) * scale).astype(jnp.bfloat16)
    scores_f32 = grad_scores.astype(jnp.float32)
    grad_query = jnp.einsum('hqk,hdk->hdq', scores_f32, key_rows.astype(jnp.float32)).astype(jnp.bfloat16)
    grad_key = jnp.einsum('hqk,hdq->hdk', scores_f32, query_rows.astype(jnp.float32)).astype(jnp.bfloat16)
    grad_value = jnp.einsum('hqk,hdq->hdk', probs_f32, grad_attn.astype(jnp.float32)).astype(jnp.bfloat16)
    return (attended, grad_query, grad_key, grad_value)

def reference(features, conv_weight, qkv_weight, out_weight, cotangent, neighbours, send_slot, recv_slot):
    present = neighbours >= 0
    cell_ids = jnp.arange(NCELL, dtype=jnp.int32)
    base_cell = cell_ids // CELLS_DEV * CELLS_DEV - FY * FZ
    gather_at = jnp.where(present, neighbours + base_cell[None, :], 0).astype(jnp.int32)
    zero_bf = jnp.zeros((), jnp.bfloat16)

    def conv_step(running, pieces):
        weight_k, index_row, present_row = pieces
        columns = jnp.where(present_row[None, :], jnp.take(features, index_row, axis=1), zero_bf)
        return (running + jnp.dot(weight_k, columns, preferred_element_type=jnp.float32), None)
    conv_out, _ = lax.scan(conv_step, jnp.zeros((C, NCELL), jnp.float32), (conv_weight, gather_at, present))
    layer_one = (features.astype(jnp.float32) + conv_out).astype(jnp.bfloat16)
    owner_key = cell_ids // CELLS_DEV * PATCH + send_slot
    slot_table = jnp.zeros((N_VOX * PATCH,), jnp.int32).at[jnp.where(send_slot >= 0, owner_key, N_VOX * PATCH)].set(cell_ids, mode='drop')
    position = jnp.arange(NH, dtype=jnp.int32)
    live_mask = recv_slot >= 0
    safe_slot = jnp.maximum(recv_slot, 0).astype(jnp.int32)
    source_cell = slot_table[safe_slot // CAP * PATCH + position // PATCH * CAP + safe_slot % CAP].astype(jnp.int32)
    grouped = jnp.where(live_mask[None, :], jnp.take(layer_one, source_cell, axis=1), zero_bf)
    grouped_f32 = grouped.astype(jnp.float32)
    col_mean = lax.optimization_barrier(jnp.mean(grouped_f32, axis=0, keepdims=True))
    centred = grouped_f32 - col_mean
    col_var = lax.optimization_barrier(jnp.mean(centred * centred, axis=0, keepdims=True))
    inverse = lax.rsqrt(col_var + 1e-05)
    normal_f32 = centred * inverse
    normed = normal_f32.astype(jnp.bfloat16)
    projected = [jnp.dot(qkv_weight[which].T, normed, preferred_element_type=jnp.float32).astype(jnp.bfloat16) for which in range(3)]
    masked_cot = jnp.where(live_mask[None, :], cotangent, zero_bf)
    grad_attn = jnp.dot(out_weight, masked_cot, preferred_element_type=jnp.float32).astype(jnp.bfloat16)

    def by_patch(array):
        return array.reshape(HEADS, C // HEADS, N_VOX, PATCH).transpose(2, 0, 1, 3)

    def from_patch(array):
        return array.transpose(1, 2, 0, 3).reshape(C, NH)

    def one_patch(pieces):
        return attend(*pieces)
    outputs = lax.map(one_patch, (by_patch(projected[0]), by_patch(projected[1]), by_patch(projected[2]), live_mask.reshape(N_VOX, PATCH), by_patch(grad_attn)))
    attended, grad_query, grad_key, grad_value = [from_patch(stacked) for stacked in outputs]
    mixed_out = jnp.dot(out_weight.T, attended, preferred_element_type=jnp.float32)
    block_out = jnp.where(live_mask[None, :], grouped_f32 + mixed_out, 0.0).astype(jnp.bfloat16)
    grad_out = jnp.dot(attended, masked_cot.T, preferred_element_type=jnp.float32)
    grad_parts = (grad_query, grad_key, grad_value)
    grad_qkv = jnp.stack([jnp.dot(normed, grad_part.T, preferred_element_type=jnp.float32) for grad_part in grad_parts])
    grad_sum = jnp.dot(qkv_weight[0], grad_query, preferred_element_type=jnp.float32)
    grad_sum = grad_sum + jnp.dot(qkv_weight[1], grad_key, preferred_element_type=jnp.float32)
    grad_sum = grad_sum + jnp.dot(qkv_weight[2], grad_value, preferred_element_type=jnp.float32)
    grad_norm_f32 = grad_sum.astype(jnp.bfloat16).astype(jnp.float32)
    grad_ln = inverse * (grad_norm_f32 - lax.optimization_barrier(jnp.mean(grad_norm_f32, axis=0, keepdims=True)) - normal_f32 * lax.optimization_barrier(jnp.mean(grad_norm_f32 * normal_f32, axis=0, keepdims=True)))
    grad_grouped = jnp.where(live_mask[None, :], masked_cot.astype(jnp.float32) + grad_ln, 0.0).astype(jnp.bfloat16)
    grad_layer = jnp.zeros((C, NCELL), jnp.bfloat16).at[:, jnp.where(live_mask, source_cell, NCELL)].set(grad_grouped, mode='drop')

    def weight_step(carry, pieces):
        index_row, present_row = pieces
        columns = jnp.where(present_row[None, :], jnp.take(features, index_row, axis=1), zero_bf)
        return (carry, jnp.dot(grad_layer, columns.T, preferred_element_type=jnp.float32))
    _, grad_conv = lax.scan(weight_step, jnp.zeros((), jnp.float32), (gather_at, present))

    def input_step(running, pieces):
        weight_k, index_row, present_row = pieces
        columns = jnp.where(present_row[None, :], jnp.take(grad_layer, index_row, axis=1), zero_bf)
        return (running + jnp.dot(weight_k.T, columns, preferred_element_type=jnp.float32), None)
    grad_features, _ = lax.scan(input_step, grad_layer.astype(jnp.float32), (conv_weight, gather_at[::-1], present[::-1]))
    return (block_out, grad_features, grad_conv, grad_qkv, grad_out)
```

```python
import jax
import jax.numpy as jnp
from jax import lax
from jax.experimental import pallas as pl
from jax.experimental.pallas import tpu as pltpu
from jax.sharding import Mesh
from jax.sharding import PartitionSpec as P

MESH = pl.DeviceIdType.MESH
VOX = ("vox_0", "vox_1", "vox_2")
BF = jnp.bfloat16
F32 = jnp.float32
CELLS = 4096
LAYER = 256
EXT = CELLS + 2 * LAYER
SLOTS = 1024
ORDER = (4, 3, 5, 2, 6, 1, 7)


def nn(a, b):
    return jnp.dot(a, b, preferred_element_type=F32)


def nt(a, b):
    return lax.dot_general(a, b, (((1,), (1,)), ((), ())), preferred_element_type=F32)


def tn(a, b):
    return lax.dot_general(a, b, (((0,), (0,)), ((), ())), preferred_element_type=F32)


def lanes(shape):
    return lax.broadcasted_iota(jnp.int32, shape, 1)


def swap_blocks(tiles):
    flat = tiles.reshape(128, 128)
    turned = [flat if s == 0 else pltpu.roll(flat, s * 16, 1) for s in range(8)]
    block = lanes((16, 128)) // 16
    out = []
    for j in range(8):
        tile = turned[(0 - j) % 8][0:16]
        for i in range(1, 8):
            tile = jnp.where(block == i, turned[(i - j) % 8][i * 16 : i * 16 + 16], tile)
        out.append(tile)
    return out


def in_layer(width, dy, dz):
    cell = lanes((16, width))
    row = (cell // 16) % 16 + dy
    col = cell % 16 + dz
    return (row >= 0) & (row < 16) & (col >= 0) & (col < 16)


def whole_kernel(
    f_ref, ss_ref, rs_ref, cot_ref, wb_ref, w2_ref, ow_ref,
    bo_ref, gf_ref, vv_ref,
    onehot, pick, fx, hx, hl, fm, wt, aw, w9, s9, layer, s1, a1, t1, a2, gw, cw, mine2, ww,
    kvt, qg, pk, acc, big, bsl, xs, ys, u1, c2, v1, d1, glw, gx, hf, hl2, hg,
    vs, e0, e1s, e2, f0, fz, f1, vg,
    ring_s, ring_r, ex_s, ex_r, halo_s, halo_r,
):
    z = lax.axis_index("vox_0")
    xc = lax.axis_index("vox_1") * 2 + lax.axis_index("vox_2")
    y = lax.axis_index("ch")
    d = z * 8 + xc

    def to_y(p):
        return {"ch": p}

    def to_z(p):
        return {"vox_0": p}

    def to_xc(p):
        return {"vox_1": p // 2, "vox_2": lax.rem(p, 2)}

    def to_d(p):
        return {"vox_0": p // 8, "vox_1": lax.rem(p, 8) // 2, "vox_2": lax.rem(p, 2)}

    after, before = lax.rem(d + 1, 64), lax.rem(d + 63, 64)

    barrier = pltpu.get_barrier_semaphore()
    for r in range(1, 8):
        for me, where in ((y, to_y), (z, to_z), (xc, to_xc)):
            pl.semaphore_signal(
                barrier, inc=1, device_id=where(lax.rem(me + r, 8)), device_id_type=MESH
            )
    for p in (after, before):
        pl.semaphore_signal(barrier, inc=1, device_id=to_d(p), device_id_type=MESH)

    sent = []

    def send(src, dst, s_sem, r_sem, where):
        copy = pltpu.make_async_remote_copy(
            src_ref=src, dst_ref=dst, send_sem=s_sem, recv_sem=r_sem,
            device_id=where, device_id_type=MESH,
        )
        copy.start()
        sent.append(copy)
        return copy

    def exchange(phase, me, where, src_of, dst):
        copies = []
        for r in ORDER:
            p = lax.rem(me + r, 8)
            copies.append(
                send(src_of(p), dst, ex_s.at[phase, r], ex_r.at[phase, r], where(p))
            )
        return copies

    def arrive(copies):
        for copy in copies:
            copy.wait_recv()

    def rows16(b):
        return pl.ds(pl.multiple_of(b * 16, 16), 16)

    def tile(b):
        return pl.ds(pl.multiple_of(b * 128, 128), 128)

    mine = rows16(y)
    ss = ss_ref[...]
    occupied = ss >= 0
    live = rs_ref[...] >= 0

    own = jnp.where(occupied, f_ref[...].astype(F32), 0.0).astype(BF)
    fm[...] = own
    fx[mine, LAYER : LAYER + CELLS] = own
    weights = jnp.concatenate([wb_ref[...].astype(F32), jnp.zeros((80, 128), F32)], axis=0)
    for t in range(4):
        wt[:, t * 128 : t * 128 + 128] = weights[t * 128 : t * 128 + 128, :].T.astype(BF)
    cw[mine, :] = jnp.where(live, cot_ref[...].astype(F32), 0.0).astype(BF)
    mine2[0:48, :] = w2_ref[...]
    mine2[48:64, :] = ow_ref[...]
    ww[y] = mine2[...]
    aw[y] = wt[mine, :]

    pl.semaphore_wait(barrier, 23)

    halo = [
        send(fm.at[:, CELLS - LAYER : CELLS], hl.at[0], halo_s.at[0], halo_r.at[0], to_d(after)),
        send(fm.at[:, 0:LAYER], hl.at[1], halo_s.at[1], halo_r.at[1], to_d(before)),
    ]

    def onehot_piece(piece):
        def step(i, carry):
            at = pl.multiple_of(piece * 64 + i * 16, 16)
            ids = lax.broadcasted_iota(jnp.int32, (16, CELLS), 0) + at
            onehot[pl.ds(at, 16), :] = jnp.where(ids == ss, 1.0, 0.0).astype(BF)
            return carry

        lax.fori_loop(0, 4, step, 0)

    source = rs_ref[...]
    route = (source >> 4) & 7
    spot = jnp.where(live, route * 128 + ((source >> 7) & 7) * 16 + (source & 15), -1)

    def pick_piece(piece):
        def step(i, carry):
            at = pl.multiple_of(piece * 256 + i * 16, 16)
            ids = lax.broadcasted_iota(jnp.int32, (16, SLOTS), 0) + at
            pick[pl.ds(at, 16), :] = jnp.where(ids == spot, 1.0, 0.0).astype(BF)
            return carry

        lax.fori_loop(0, 16, step, 0)

    work = [lambda i=i: onehot_piece(i) for i in range(16)]
    work += [lambda i=i: pick_piece(i) for i in range(4)]

    def chunk_of(c):
        if c < 4:
            return lambda b: fx.at[rows16(b), LAYER + c * 1024 : LAYER + c * 1024 + 1024]
        return lambda b: hx.at[rows16(b), :]

    chunks = [chunk_of(c) for c in range(5)]
    hops = ((4, 4, 3, 3, 4), (3, 3, 4, 4, 3))
    ring = {}
    for s in range(4):
        for c in range(5):
            if s == 0 and c == 4:
                arrive(halo)
                left = jnp.where(d == 0, 0.0, hl[0].astype(F32)).astype(BF)
                right = jnp.where(d == 63, 0.0, hl[1].astype(F32)).astype(BF)
                hx[mine, 0:LAYER] = left
                hx[mine, LAYER : 2 * LAYER] = right
            if s > 0 and work:
                work.pop(0)()
            for way in range(2):
                if s >= hops[way][c]:
                    continue
                if s > 0:
                    ring[way, s - 1, c].wait_recv()
                block = lax.rem(y + 8 - s, 8) if way == 0 else lax.rem(y + s, 8)
                to = lax.rem(y + 1, 8) if way == 0 else lax.rem(y + 7, 8)
                ring[way, s, c] = send(
                    chunks[c](block), chunks[c](block),
                    ring_s.at[way, s, c], ring_r.at[way, s, c], to_y(to),
                )
        if s == 0:
            got_aw = exchange(0, y, to_y, lambda p: wt.at[rows16(p), :], aw.at[y])
    while work:
        work.pop(0)()
    for c in range(5):
        for way in range(2):
            ring[way, hops[way][c] - 1, c].wait_recv()
    got_ww = exchange(1, y, to_y, lambda p: mine2, ww.at[y])
    got_cw = exchange(2, y, to_y, lambda p: cw.at[mine, :], cw.at[mine, :])
    fx[:, 0:LAYER] = hx[:, 0:LAYER]
    fx[:, LAYER + CELLS : EXT] = hx[:, LAYER : 2 * LAYER]

    arrive(got_aw)
    for t in range(4):
        for k, part in enumerate(swap_blocks(aw[:, :, t * 128 : t * 128 + 128].astype(F32))):
            if t * 8 + k < 27:
                at = (t * 8 + k) * 16
                w9[at : at + 16, :] = part.astype(BF)

    taps = [(dy, dz) for dy in (-1, 0, 1) for dz in (-1, 0, 1)]

    def conv_step(i, carry):
        total = None
        for dx in range(3):
            field = fx[:, pl.ds(pl.multiple_of(i * 512 + dx * LAYER, LAYER), 512)]
            term = nn(w9[dx * 144 : dx * 144 + 144, :], field)
            total = term if total is None else total + term
        out = fm[:, pl.ds(pl.multiple_of(i * 512, 512), 512)].astype(F32)
        conv = jnp.zeros((16, 512), F32)
        for j, (dy, dz) in enumerate(taps):
            shift = -(dy * 16 + dz) % 512
            slab = total[j * 16 : j * 16 + 16]
            slab = pltpu.roll(slab, shift, 1) if shift else slab
            conv = conv + jnp.where(in_layer(512, dy, dz), slab, 0.0)
        layer[:, pl.ds(pl.multiple_of(i * 512, 512), 512)] = (out + conv).astype(BF)
        return carry

    lax.fori_loop(0, 8, conv_step, 0)

    def pack_step(i, carry):
        rows = nt(layer[...], onehot[pl.ds(pl.multiple_of(i * 256, 256), 256), :])
        s1[2 * i] = rows[:, 0:128].astype(BF)
        s1[2 * i + 1] = rows[:, 128:256].astype(BF)
        return carry

    lax.fori_loop(0, 4, pack_step, 0)
    a1[z] = s1[z]
    got = exchange(3, z, to_z, lambda p: s1.at[p], a1.at[z])

    def shifted_step(i, carry):
        at = pl.ds(pl.multiple_of(i * 512, 512), 512)
        x = fx[mine, at].astype(F32)
        for j, (dy, dz) in enumerate(taps):
            shift = -(dy * 16 + dz) % 512
            slab = pltpu.roll(x, shift, 1) if shift else x
            s9[j * 16 : j * 16 + 16, at] = jnp.where(in_layer(512, dy, dz), slab, 0.0).astype(BF)
        return carry

    lax.fori_loop(0, EXT // 512, shifted_step, 0)

    arrive(got)
    for j, part in enumerate(swap_blocks(a1[...].astype(F32))):
        t1[j] = part.astype(BF)
    a2[xc] = t1[xc]
    got = exchange(4, xc, to_xc, lambda p: t1.at[p], a2.at[xc])
    arrive(got)
    arrived = jnp.concatenate([a2[i] for i in range(8)], axis=1)
    gw[mine, :] = nn(arrived, pick[...]).astype(BF)
    got = exchange(5, y, to_y, lambda p: gw.at[mine, :], gw.at[mine, :])
    arrive(got_cw)
    arrive(got_ww)
    ga = nn(ow_ref[...], cw[...]).astype(BF)
    arrive(got)

    whole = gw[...].astype(F32)
    mean = jnp.mean(whole, axis=0, keepdims=True)
    centred = whole - mean
    var = jnp.mean(centred * centred, axis=0, keepdims=True)
    normed = (centred * lax.rsqrt(var + 1e-05)).astype(BF)
    big[...] = normed
    qkv = nn(w2_ref[...], normed).astype(BF)
    quarter = (qkv[0:16].astype(F32) * 0.25).astype(BF)
    row = lax.broadcasted_iota(jnp.int32, (16, SLOTS), 0)
    bias = jnp.where((row == 0) & (~live), -1e30, 0.0)
    stacked = jnp.concatenate(
        [
            qkv[16:32].astype(F32),
            bias,
            qkv[32:48].astype(F32),
            jnp.zeros((80, SLOTS), F32),
        ],
        axis=0,
    )
    for t in range(8):
        kvt[t * 128 : t * 128 + 128, :] = stacked[:, t * 128 : t * 128 + 128].T.astype(BF)
    ones = jnp.where(lax.broadcasted_iota(jnp.int32, (16, 128), 0) == 0, 1.0, 0.0).astype(BF)
    for t in range(8):
        cols = slice(t * 128, t * 128 + 128)
        left = jnp.concatenate([quarter[:, cols], ones, jnp.zeros((96, 128), BF)], axis=0)
        right = jnp.concatenate(
            [jnp.zeros((32, 128), BF), ga[:, cols], jnp.zeros((80, 128), BF)], axis=0
        )
        qg[t] = jnp.concatenate([left, right], axis=1)
    vk = jnp.concatenate([qkv[32:48], qkv[16:32]], axis=0)
    mixed_rows = []
    for t in range(8):
        cols = slice(t * 128, t * 128 + 128)
        zero = jnp.zeros((16, 128), BF)
        mixed_rows.append(
            jnp.concatenate(
                [
                    jnp.concatenate([zero, qkv[0:16, cols]], axis=1),
                    jnp.concatenate([ga[:, cols], zero], axis=1),
                ],
                axis=0,
            )
        )
    for t in range(8):
        bsl[t] = mixed_rows[t]
    acc[...] = jnp.zeros((32, SLOTS), F32)

    def attend_step(i, carry):
        both = nn(kvt[...], qg[i])
        logits, grad_logits = both[:, 0:128], both[:, 128:256]
        exponents = jnp.exp(logits - jnp.max(logits, axis=0, keepdims=True))
        total = jnp.sum(exponents, axis=0, keepdims=True)
        probs = (exponents * (1.0 / total)).astype(BF)
        wide = probs.astype(F32)
        inner = jnp.sum(wide * grad_logits, axis=0, keepdims=True)
        scores = (wide * (grad_logits - inner) * 0.25).astype(BF)
        pair = jnp.concatenate([probs, scores], axis=1)
        near = nn(vk, pair)
        at = tile(i)
        pk[0:16, at] = near[0:16, 0:128].astype(BF)
        pk[16:32, at] = near[16:32, 128:256].astype(BF)
        acc[...] += nt(bsl[i], pair)
        return carry

    lax.fori_loop(0, 8, attend_step, 0)
    pk[32:64, :] = acc[...].astype(BF)

    ys[y] = pk[:, tile(y)]
    got = exchange(6, y, to_y, lambda p: pk.at[:, tile(p)], ys.at[y])
    vs[432:480, :] = nt(pk[16:64, :], big[...])
    vs[480:496, :] = nt(pk[0:16, :], cw[...])
    vs[496:512, :] = jnp.zeros((16, 128), F32)
    own_slots = tile(y)
    part = gw[:, own_slots].astype(F32)
    mean = jnp.mean(part, axis=0, keepdims=True)
    centred = part - mean
    var = jnp.mean(centred * centred, axis=0, keepdims=True)
    inverse = lax.rsqrt(var + 1e-05)
    normal = centred * inverse
    cot = cw[:, own_slots].astype(F32)
    live_part = rs_ref[:, own_slots] >= 0
    arrive(got)
    mixed = tn(ww[:, 48:64, :].reshape(128, 128), ys[:, 0:16, :].reshape(128, 128))
    grad = None
    for i in range(3):
        term = tn(
            ww[:, i * 16 : i * 16 + 16, :].reshape(128, 128),
            ys[:, 16 + i * 16 : 32 + i * 16, :].reshape(128, 128),
        )
        grad = term if grad is None else grad + term
    grad = grad.astype(BF).astype(F32)
    grad_ln = inverse * (
        grad
        - jnp.mean(grad, axis=0, keepdims=True)
        - normal * jnp.mean(grad * normal, axis=0, keepdims=True)
    )
    back = jnp.where(live_part, cot + grad_ln, 0.0).astype(BF)
    block = jnp.where(live_part, part + mixed, 0.0).astype(BF)
    xs[:, 0:16, :] = back.reshape(8, 16, 128)
    xs[:, 16:32, :] = block.reshape(8, 16, 128)
    u1[y] = xs[y]
    got = exchange(7, y, to_y, lambda p: xs.at[p], u1.at[y])
    arrive(got)
    grad_grouped = jnp.concatenate([u1[i, 0:16] for i in range(8)], axis=1)
    spread = nt(grad_grouped, pick[...])
    for t in range(8):
        c2[t] = spread[:, t * 128 : t * 128 + 128].astype(BF)
    v1[xc] = c2[xc]
    got = exchange(8, xc, to_xc, lambda p: c2.at[p], v1.at[xc])
    bo_ref[...] = jnp.concatenate([u1[i, 16:32] for i in range(8)], axis=1)
    arrive(got)
    for j, piece in enumerate(swap_blocks(v1[...].astype(F32))):
        d1[j] = piece.astype(BF)
    e0[z] = d1[z]
    got = exchange(9, z, to_z, lambda p: d1.at[p], e0.at[z])
    arrive(got)
    slots = jnp.concatenate([e0[i] for i in range(8)], axis=1)
    glw[mine, :] = slots
    got = exchange(10, y, to_y, lambda p: glw.at[mine, :], glw.at[mine, :])
    hf[:, 0:LAYER] = nn(slots, onehot[:, 0:LAYER]).astype(BF)
    hf[:, LAYER : 2 * LAYER] = nn(slots, onehot[:, CELLS - LAYER : CELLS]).astype(BF)
    halo = [
        send(hf.at[:, LAYER : 2 * LAYER], hl2.at[0], halo_s.at[2], halo_r.at[2], to_d(after)),
        send(hf.at[:, 0:LAYER], hl2.at[1], halo_s.at[3], halo_r.at[3], to_d(before)),
    ]
    arrive(halo)
    hg[mine, 0:LAYER] = jnp.where(d == 0, 0.0, hl2[0].astype(F32)).astype(BF)
    hg[mine, LAYER : 2 * LAYER] = jnp.where(d == 63, 0.0, hl2[1].astype(F32)).astype(BF)
    got_halo = exchange(11, y, to_y, lambda p: hg.at[mine, :], hg.at[mine, :])
    arrive(got)

    def expand_step(i, carry):
        at = pl.multiple_of(i * 512, 512)
        gx[:, pl.ds(pl.multiple_of(at + LAYER, LAYER), 512)] = nn(
            glw[...], onehot[:, pl.ds(at, 512)]
        ).astype(BF)
        return carry

    lax.fori_loop(0, 8, expand_step, 0)

    for dx in range(3):
        vs[dx * 144 : dx * 144 + 144, :] = nt(
            s9[:, dx * LAYER : dx * LAYER + CELLS], gx[:, LAYER : LAYER + CELLS]
        )

    def rows64(b):
        return pl.ds(pl.multiple_of(b * 64, 64), 64)

    def rows8(b):
        return pl.ds(pl.multiple_of(b * 8, 8), 8)

    e1s[xc] = vs[rows64(xc), :]
    got = exchange(12, xc, to_xc, lambda p: vs.at[rows64(p), :], e1s.at[xc])

    arrive(got_halo)
    gx[:, 0:LAYER] = hg[:, 0:LAYER]
    gx[:, LAYER + CELLS : EXT] = hg[:, LAYER : 2 * LAYER]

    def input_step(i, carry):
        total = None
        for dx in range(3):
            field = gx[:, pl.ds(pl.multiple_of(i * 512 + (2 - dx) * LAYER, LAYER), 512)]
            term = nn(wb_ref[dx * 144 : dx * 144 + 144, :], field)
            total = term if total is None else total + term
        at = pl.ds(pl.multiple_of(i * 512, 512), 512)
        conv = jnp.zeros((16, 512), F32)
        for j, (dy, dz) in enumerate(taps):
            shift = (dy * 16 + dz) % 512
            slab = total[j * 16 : j * 16 + 16]
            slab = pltpu.roll(slab, shift, 1) if shift else slab
            conv = conv + jnp.where(in_layer(512, -dy, -dz), slab, 0.0)
        own_grad = gx[mine, pl.ds(pl.multiple_of(i * 512 + LAYER, LAYER), 512)].astype(F32)
        gf_ref[:, at] = own_grad + jnp.where(ss_ref[:, at] >= 0, conv, 0.0)
        return carry

    lax.fori_loop(0, 4, input_step, 0)
    arrive(got)
    total = e1s[0]
    for i in range(1, 8):
        total = total + e1s[i]
    e2[...] = total
    f0[z] = e2[rows8(z), :]
    got = exchange(13, z, to_z, lambda p: e2.at[rows8(p), :], f0.at[z])
    lax.fori_loop(4, 8, input_step, 0)
    arrive(got)
    total = f0[0]
    for i in range(1, 8):
        total = total + f0[i]
    f1[...] = total
    fz[rows8(z), :] = total
    arrive(exchange(14, z, to_z, lambda p: f1, fz.at[rows8(z), :]))
    vg[rows64(xc), :] = fz[...]
    arrive(exchange(15, xc, to_xc, lambda p: fz, vg.at[rows64(xc), :]))
    vv_ref[...] = vg[...]
    for copy in sent:
        copy.wait_send()


def body(
    features, conv_weight, qkv_weight, out_weight, cotangent, neighbours, send_slot, recv_slot
):
    wb = jnp.transpose(conv_weight, (0, 2, 1)).reshape(432, 128)
    w2 = jnp.transpose(qkv_weight, (0, 2, 1)).reshape(48, 128)
    vmem = pl.BlockSpec(memory_space=pltpu.VMEM)

    def buf(*shape):
        return pltpu.VMEM(shape, BF)

    def wide(*shape):
        return pltpu.VMEM(shape, F32)

    scratch = [
        buf(SLOTS, CELLS), buf(SLOTS, SLOTS),
        buf(128, EXT), buf(128, 512), buf(2, 16, LAYER), buf(16, CELLS),
        buf(128, 512), buf(8, 16, 512), buf(432, 128), buf(144, EXT),
        buf(16, CELLS), buf(8, 16, 128), buf(8, 16, 128), buf(8, 16, 128), buf(8, 16, 128),
        buf(128, SLOTS), buf(128, SLOTS), buf(64, 128), buf(8, 64, 128),
        buf(SLOTS, 128), buf(8, 128, 256), buf(64, SLOTS), wide(32, SLOTS),
        buf(128, SLOTS), buf(8, 32, 256), buf(8, 32, 128), buf(8, 64, 128),
        buf(8, 32, 128), buf(8, 16, 128), buf(8, 16, 128), buf(8, 16, 128),
        buf(128, SLOTS), buf(128, EXT), buf(16, 512), buf(2, 16, LAYER), buf(128, 512),
        wide(512, 128), buf(8, 16, 128), wide(8, 64, 128), wide(64, 128),
        wide(8, 8, 128), wide(64, 128), wide(8, 128), wide(512, 128),
        pltpu.SemaphoreType.DMA((2, 4, 5)), pltpu.SemaphoreType.DMA((2, 4, 5)),
        pltpu.SemaphoreType.DMA((16, 8)), pltpu.SemaphoreType.DMA((16, 8)),
        pltpu.SemaphoreType.DMA((4,)), pltpu.SemaphoreType.DMA((4,)),
    ]
    block_out, grad_features, sums = pl.pallas_call(
        whole_kernel,
        out_shape=(
            jax.ShapeDtypeStruct((16, SLOTS), BF),
            jax.ShapeDtypeStruct((16, CELLS), F32),
            jax.ShapeDtypeStruct((512, 128), F32),
        ),
        in_specs=[vmem] * 7,
        out_specs=(vmem, vmem, vmem),
        scratch_shapes=scratch,
        compiler_params=pltpu.CompilerParams(
            collective_id=0, has_side_effects=True, vmem_limit_bytes=48 * 1024 * 1024
        ),
    )(
        features, send_slot.reshape(1, CELLS), recv_slot.reshape(1, SLOTS), cotangent,
        wb, w2, out_weight,
    )
    grad_conv = jnp.transpose(sums[0:432].reshape(27, 16, 128), (0, 2, 1))
    grad_qkv = jnp.transpose(sums[432:480].reshape(3, 16, 128), (0, 2, 1))
    return (block_out, grad_features, grad_conv, grad_qkv, sums[480:496])


def solution(mesh):
    torus = Mesh(mesh.devices.reshape(8, 4, 2, mesh.shape["ch"]), ("vox_0", "vox_1", "vox_2", "ch"))
    placed = (
        P("ch", VOX),
        P(None, None, "ch"),
        P(None, None, "ch"),
        P("ch", None),
        P("ch", VOX),
        P(None, VOX),
        P(VOX),
        P(VOX),
    )
    return jax.shard_map(
        body,
        mesh=torus,
        in_specs=placed,
        out_specs=(
            P("ch", VOX),
            P("ch", VOX),
            P(None, None, "ch"),
            P(None, None, "ch"),
            P("ch", None),
        ),
        check_vma=False,
    )
```

```python
import jax
import jax.numpy as jnp
from jax import lax
from jax.experimental import pallas as pl
from jax.experimental.pallas import tpu as pltpu
from jax.sharding import Mesh
from jax.sharding import PartitionSpec as P

MESH = pl.DeviceIdType.MESH
VOX = ("vox_0", "vox_1", "vox_2")
BF = jnp.bfloat16
F32 = jnp.float32
CELLS = 4096
LAYER = 256
EXT = CELLS + 2 * LAYER
SLOTS = 1024
ORDER = (4, 3, 5, 2, 6, 1, 7)


def nn(a, b):
    return jnp.dot(a, b, preferred_element_type=F32)


def nt(a, b):
    return lax.dot_general(a, b, (((1,), (1,)), ((), ())), preferred_element_type=F32)


def tn(a, b):
    return lax.dot_general(a, b, (((0,), (0,)), ((), ())), preferred_element_type=F32)


def lanes(shape):
    return lax.broadcasted_iota(jnp.int32, shape, 1)


def swap_blocks(tiles):
    flat = tiles.reshape(128, 128)
    turned = [flat if s == 0 else pltpu.roll(flat, s * 16, 1) for s in range(8)]
    block = lanes((16, 128)) // 16
    out = []
    for j in range(8):
        tile = turned[(0 - j) % 8][0:16]
        for i in range(1, 8):
            tile = jnp.where(block == i, turned[(i - j) % 8][i * 16 : i * 16 + 16], tile)
        out.append(tile)
    return out


def in_layer(width, dy, dz):
    cell = lanes((16, width))
    row = (cell // 16) % 16 + dy
    col = cell % 16 + dz
    return (row >= 0) & (row < 16) & (col >= 0) & (col < 16)


def whole_kernel(
    f_in, ss_in, rs_in, cot_in, wb_in, w2_in, ow_in,
    bo_out, gf_out, vv_out,
    bo_ref, gf_ref, vv_ref, f_ref, ss_ref, rs_ref, cot_ref, wb_ref, w2_ref, ow_ref,
    onehot, pick, fx, hx, hl, fm, fc, wt, aw, w9, s27, s9c, layer, s1acc,
    s1, a1, t1, a2, gw, cw, mine2, ww,
    kvt, qq, gg, qkv, gaw, lg, pr, sc, pk, acc, big, xs, ys, u1, c2, v1, d1,
    glw, gx, hf, hl2, hg, vs, e0, half, pair, quad, own64, zsrc, zall, back64, back256,
    in_sem, out_sem, ex_s, ex_r, halo_s, halo_r, red_s, red_r,
):
    z = lax.axis_index("vox_0")
    x = lax.axis_index("vox_1")
    core = lax.axis_index("vox_2")
    xc = x * 2 + core
    y = lax.axis_index("ch")
    d = z * 8 + xc

    def to_y(p):
        return {"ch": p}

    def to_z(p):
        return {"vox_0": p}

    def to_x(p):
        return {"vox_1": p}

    def to_xc(p):
        return {"vox_1": p // 2, "vox_2": lax.rem(p, 2)}

    def to_d(p):
        return {"vox_0": p // 8, "vox_1": lax.rem(p, 8) // 2, "vox_2": lax.rem(p, 2)}

    after, before = lax.rem(d + 1, 64), lax.rem(d + 63, 64)

    barrier = pltpu.get_barrier_semaphore()
    for r in range(1, 8):
        for me, where in ((y, to_y), (z, to_z), (xc, to_xc)):
            pl.semaphore_signal(
                barrier, inc=1, device_id=where(lax.rem(me + r, 8)), device_id_type=MESH
            )
    for p in (after, before):
        pl.semaphore_signal(barrier, inc=1, device_id=to_d(p), device_id_type=MESH)

    loads = [
        pltpu.make_async_copy(src, dst, in_sem.at[i])
        for i, (src, dst) in enumerate(
            (
                (ss_in, ss_ref), (f_in, f_ref), (wb_in, wb_ref), (rs_in, rs_ref),
                (cot_in, cot_ref), (w2_in, w2_ref), (ow_in, ow_ref),
            )
        )
    ]
    for load in loads:
        load.start()

    fresh, old = [], []

    def send(src, dst, s_sem, r_sem, where):
        copy = pltpu.make_async_remote_copy(
            src_ref=src, dst_ref=dst, send_sem=s_sem, recv_sem=r_sem,
            device_id=where, device_id_type=MESH,
        )
        copy.start()
        fresh.append(copy)
        return copy

    def drain():
        for copy in old:
            copy.wait_send()
        old[:] = fresh
        fresh.clear()

    def exchange(phase, me, where, src_of, dst):
        copies = []
        for r in ORDER:
            p = lax.rem(me + r, 8)
            copies.append(
                send(src_of(p), dst, ex_s.at[phase, r], ex_r.at[phase, r], where(p))
            )
        return copies

    def arrive(copies):
        for copy in copies:
            copy.wait_recv()

    def rows16(b):
        return pl.ds(pl.multiple_of(b * 16, 16), 16)

    def tile(b):
        return pl.ds(pl.multiple_of(b * 128, 128), 128)

    def span(i, start=0, size=512):
        return pl.ds(pl.multiple_of(i * 512 + start, 256), size)

    mine = rows16(y)
    loads[0].wait()

    def onehot_step(i, carry):
        at = pl.multiple_of(i * 16, 16)
        ids = lax.broadcasted_iota(jnp.int32, (16, CELLS), 0) + at
        onehot[pl.ds(at, 16), :] = jnp.where(ids == ss_ref[...], 1.0, 0.0).astype(BF)
        return carry

    lax.fori_loop(0, 64, onehot_step, 0)

    loads[1].wait()
    fm[...] = jnp.where(ss_ref[...] >= 0, f_ref[...].astype(F32), 0.0).astype(BF)

    def compact_step(i, carry):
        at = pl.multiple_of(i * 256, 256)
        fc[mine, pl.ds(at, 256)] = nt(fm[...], onehot[pl.ds(at, 256), :]).astype(BF)
        return carry

    lax.fori_loop(0, 4, compact_step, 0)

    loads[2].wait()
    weights = jnp.concatenate([wb_ref[...].astype(F32), jnp.zeros((80, 128), F32)], axis=0)
    for t in range(4):
        wt[:, t * 128 : t * 128 + 128] = weights[t * 128 : t * 128 + 128, :].T.astype(BF)

    pl.semaphore_wait(barrier, 23)
    got = exchange(0, y, to_y, lambda p: fc.at[mine, :], fc.at[mine, :])
    halo = [
        send(fm.at[:, CELLS - LAYER : CELLS], hl.at[0], halo_s.at[0], halo_r.at[0], to_d(after)),
        send(fm.at[:, 0:LAYER], hl.at[1], halo_s.at[1], halo_r.at[1], to_d(before)),
    ]
    got_aw = exchange(11, y, to_y, lambda p: wt.at[rows16(p), :], aw.at[y])

    aw[y] = wt[mine, :]
    for load in loads[3:]:
        load.wait()
    live = rs_ref[...] >= 0
    cw[mine, :] = jnp.where(live, cot_ref[...].astype(F32), 0.0).astype(BF)
    mine2[0:48, :] = w2_ref[...]
    mine2[48:64, :] = ow_ref[...]
    ww[y] = mine2[...]
    source = rs_ref[...]
    route = (source >> 4) & 7
    spot = jnp.where(live, route * 128 + ((source >> 7) & 7) * 16 + (source & 15), -1)

    arrive(halo)
    hx[mine, 0:LAYER] = jnp.where(d == 0, 0.0, hl[0].astype(F32)).astype(BF)
    hx[mine, LAYER : 2 * LAYER] = jnp.where(d == 63, 0.0, hl[1].astype(F32)).astype(BF)
    got_hx = exchange(12, y, to_y, lambda p: hx.at[mine, :], hx.at[mine, :])

    taps = [(dy, dz) for dy in (-1, 0, 1) for dz in (-1, 0, 1)]

    def shifted(values, width, put):
        for j, (dy, dz) in enumerate(taps):
            shift = -(dy * 16 + dz) % width
            slab = pltpu.roll(values, shift, 1) if shift else values
            slab = jnp.where(in_layer(width, dy, dz), slab, 0.0).astype(BF)
            for dx in range(3):
                put(dx, dx * 144 + j * 16, slab)

    def shifted_step(i, carry):
        def put(dx, row, slab):
            s27[row : row + 16, span(i, (3 - dx) * LAYER)] = slab

        shifted(fm[:, span(i)].astype(F32), 512, put)
        return carry

    lax.fori_loop(0, 8, shifted_step, 0)
    edges = hx[mine, :].astype(F32)

    def put_left(dx, row, slab):
        s27[row : row + 16, (2 - dx) * LAYER : (3 - dx) * LAYER] = slab[:, 0:LAYER]

    def put_right(dx, row, slab):
        s27[row : row + 16, (19 - dx) * LAYER : (20 - dx) * LAYER] = slab[:, LAYER : 2 * LAYER]

    shifted(edges, 512, put_left)
    shifted(edges, 512, put_right)

    def s9c_step(i, carry):
        at = pl.multiple_of(i * 256, 256)
        s9c[:, pl.ds(at, 256)] = nt(
            s27[:, 512 : 512 + CELLS], onehot[pl.ds(at, 256), :]
        ).astype(BF)
        return carry

    lax.fori_loop(0, 4, s9c_step, 0)

    def pick_step(i, carry):
        at = pl.multiple_of(i * 16, 16)
        ids = lax.broadcasted_iota(jnp.int32, (16, SLOTS), 0) + at
        pick[pl.ds(at, 16), :] = jnp.where(ids == spot, 1.0, 0.0).astype(BF)
        return carry

    lax.fori_loop(0, 64, pick_step, 0)
    qq[...] = jnp.zeros((128, SLOTS), BF)
    gg[...] = jnp.zeros((128, SLOTS), BF)
    s1acc[...] = jnp.zeros((16, SLOTS), F32)
    acc[...] = jnp.zeros((32, SLOTS), F32)

    arrive(got_aw)
    for t in range(4):
        for k, part in enumerate(swap_blocks(aw[:, :, t * 128 : t * 128 + 128].astype(F32))):
            if t * 8 + k < 27:
                at = (t * 8 + k) * 16
                w9[at : at + 16, :] = part.astype(BF)

    arrive(got)
    got_ww = exchange(1, y, to_y, lambda p: mine2, ww.at[y])
    got_cw = exchange(2, y, to_y, lambda p: cw.at[mine, :], cw.at[mine, :])
    drain()

    def expand(src, dst, i):
        dst[:, span(i, LAYER)] = nn(src[...], onehot[:, span(i)]).astype(BF)

    def conv(i):
        total = None
        for dx in range(3):
            field = fx[:, span(i, dx * LAYER)]
            term = nn(w9[dx * 144 : dx * 144 + 144, :], field)
            total = term if total is None else total + term
        out = fm[:, span(i)].astype(F32)
        summed = jnp.zeros((16, 512), F32)
        for j, (dy, dz) in enumerate(taps):
            shift = -(dy * 16 + dz) % 512
            slab = total[j * 16 : j * 16 + 16]
            slab = pltpu.roll(slab, shift, 1) if shift else slab
            summed = summed + jnp.where(in_layer(512, dy, dz), slab, 0.0)
        layer[:, span(i)] = (out + summed).astype(BF)

    def pack(i):
        s1acc[...] += nt(layer[:, span(i)], onehot[:, span(i)])

    for i in range(3):
        expand(fc, fx, i)
    arrive(got_hx)
    fx[:, 0:LAYER] = hx[:, 0:LAYER]
    fx[:, LAYER + CELLS : EXT] = hx[:, LAYER : 2 * LAYER]
    conv(0)

    def conv_step(i, carry):
        pack(i - 1)
        conv(i)
        expand(fc, fx, i + 2)
        return carry

    lax.fori_loop(1, 6, conv_step, 0)
    pack(5)
    conv(6)
    pack(6)
    conv(7)
    pack(7)
    packed = s1acc[...].astype(BF)
    for t in range(8):
        s1[t] = packed[:, t * 128 : t * 128 + 128]
    a1[z] = s1[z]
    got = exchange(3, z, to_z, lambda p: s1.at[p], a1.at[z])

    drain()
    arrive(got)
    for j, part in enumerate(swap_blocks(a1[...].astype(F32))):
        t1[j] = part.astype(BF)
    a2[xc] = t1[xc]
    got = exchange(4, xc, to_xc, lambda p: t1.at[p], a2.at[xc])
    drain()
    arrive(got)
    arrived = jnp.concatenate([a2[i] for i in range(8)], axis=1)
    gw[mine, :] = nn(arrived, pick[...]).astype(BF)
    got = exchange(5, y, to_y, lambda p: gw.at[mine, :], gw.at[mine, :])
    drain()
    arrive(got_cw)
    arrive(got_ww)
    ga = nn(ow_ref[...], cw[...]).astype(BF)
    gaw[...] = ga
    gg[32:48, :] = (ga.astype(F32) * 0.25).astype(BF)
    arrive(got)

    whole = gw[...].astype(F32)
    mean = jnp.mean(whole, axis=0, keepdims=True)
    centred = whole - mean
    var = jnp.mean(centred * centred, axis=0, keepdims=True)
    normed = (centred * lax.rsqrt(var + 1e-05)).astype(BF)
    big[...] = normed
    rows = nn(w2_ref[...], normed).astype(BF)
    qkv[...] = rows
    qq[0:16, :] = (rows[0:16].astype(F32) * 0.25).astype(BF)
    row = lax.broadcasted_iota(jnp.int32, (16, SLOTS), 0)
    qq[16:32, :] = jnp.where(row == 0, 1.0, 0.0).astype(BF)
    bias = jnp.where((row == 0) & (~live), -1e30, 0.0)
    stacked = jnp.concatenate(
        [
            rows[16:32].astype(F32),
            bias,
            rows[32:48].astype(F32),
            jnp.zeros((80, SLOTS), F32),
        ],
        axis=0,
    )
    for t in range(8):
        kvt[t * 128 : t * 128 + 128, :] = stacked[:, t * 128 : t * 128 + 128].T.astype(BF)

    def attend_step(i, carry):
        at = pl.ds(pl.multiple_of(i * 256, 256), 256)
        top = None
        for c in range(4):
            cells = slice(c * 256, c * 256 + 256)
            logits = nn(kvt[cells, :], qq[:, at])
            lg[cells, :] = logits
            most = jnp.max(logits.reshape(32, 8, 256), axis=0)
            top = most if top is None else jnp.maximum(top, most)
        top = jnp.max(top, axis=0, keepdims=True)
        total = jnp.zeros((8, 256), F32)
        for c in range(16):
            cells = slice(c * 64, c * 64 + 64)
            exponents = jnp.exp(lg[cells, :] - top)
            lg[cells, :] = exponents
            total = total + jnp.sum(exponents.reshape(8, 8, 256), axis=0)
        inverse_total = 1.0 / jnp.sum(total, axis=0, keepdims=True)
        for c in range(16):
            cells = slice(c * 64, c * 64 + 64)
            pr[cells, :] = (lg[cells, :] * inverse_total).astype(BF)
        attended = nn(qkv[32:48, :], pr[...])
        pk[0:16, at] = attended.astype(BF)
        inner = jnp.sum(attended * gg[32:48, at].astype(F32), axis=0, keepdims=True)
        acc[16:32, :] += nt(gaw[:, at], pr[...])
        for c in range(4):
            cells = slice(c * 256, c * 256 + 256)
            grad_logits = nn(kvt[cells, :], gg[:, at])
            sc[cells, :] = (pr[cells, :].astype(F32) * (grad_logits - inner)).astype(BF)
        pk[16:32, at] = nn(qkv[16:32, :], sc[...]).astype(BF)
        acc[0:16, :] += nt(qkv[0:16, at], sc[...])
        return carry

    lax.fori_loop(0, 4, attend_step, 0)
    pk[32:64, :] = acc[...].astype(BF)

    ys[y] = pk[:, tile(y)]
    got = exchange(6, y, to_y, lambda p: pk.at[:, tile(p)], ys.at[y])
    drain()
    vs[432:480, :] = nt(pk[16:64, :], big[...])
    vs[480:496, :] = nt(pk[0:16, :], cw[...])
    vs[496:512, :] = jnp.zeros((16, 128), F32)
    own_slots = tile(y)
    part = gw[:, own_slots].astype(F32)
    mean = jnp.mean(part, axis=0, keepdims=True)
    centred = part - mean
    var = jnp.mean(centred * centred, axis=0, keepdims=True)
    inverse = lax.rsqrt(var + 1e-05)
    normal = centred * inverse
    cot = cw[:, own_slots].astype(F32)
    live_part = rs_ref[:, own_slots] >= 0
    arrive(got)
    mixed = tn(ww[:, 48:64, :].reshape(128, 128), ys[:, 0:16, :].reshape(128, 128))
    grad = None
    for i in range(3):
        term = tn(
            ww[:, i * 16 : i * 16 + 16, :].reshape(128, 128),
            ys[:, 16 + i * 16 : 32 + i * 16, :].reshape(128, 128),
        )
        grad = term if grad is None else grad + term
    grad = grad.astype(BF).astype(F32)
    grad_ln = inverse * (
        grad
        - jnp.mean(grad, axis=0, keepdims=True)
        - normal * jnp.mean(grad * normal, axis=0, keepdims=True)
    )
    back = jnp.where(live_part, cot + grad_ln, 0.0).astype(BF)
    block = jnp.where(live_part, part + mixed, 0.0).astype(BF)
    xs[:, 0:16, :] = back.reshape(8, 16, 128)
    xs[:, 16:32, :] = block.reshape(8, 16, 128)
    u1[y] = xs[y]
    got = exchange(7, y, to_y, lambda p: xs.at[p], u1.at[y])
    drain()
    arrive(got)
    grad_grouped = jnp.concatenate([u1[i, 0:16] for i in range(8)], axis=1)
    spread = nt(grad_grouped, pick[...])
    for t in range(8):
        c2[t] = spread[:, t * 128 : t * 128 + 128].astype(BF)
    v1[xc] = c2[xc]
    got = exchange(8, xc, to_xc, lambda p: c2.at[p], v1.at[xc])
    drain()
    bo_ref[...] = jnp.concatenate([u1[i, 16:32] for i in range(8)], axis=1)
    stores = [
        pltpu.make_async_copy(src, dst, out_sem.at[i])
        for i, (src, dst) in enumerate(((bo_ref, bo_out), (gf_ref, gf_out), (vv_ref, vv_out)))
    ]
    stores[0].start()
    arrive(got)
    for j, piece in enumerate(swap_blocks(v1[...].astype(F32))):
        d1[j] = piece.astype(BF)
    e0[z] = d1[z]
    got = exchange(9, z, to_z, lambda p: d1.at[p], e0.at[z])
    drain()
    arrive(got)
    slots = jnp.concatenate([e0[i] for i in range(8)], axis=1)
    glw[mine, :] = slots
    got = exchange(10, y, to_y, lambda p: glw.at[mine, :], glw.at[mine, :])
    drain()
    hf[:, 0:LAYER] = nn(slots, onehot[:, 0:LAYER]).astype(BF)
    hf[:, LAYER : 2 * LAYER] = nn(slots, onehot[:, CELLS - LAYER : CELLS]).astype(BF)
    halo = [
        send(hf.at[:, LAYER : 2 * LAYER], hl2.at[0], halo_s.at[2], halo_r.at[2], to_d(after)),
        send(hf.at[:, 0:LAYER], hl2.at[1], halo_s.at[3], halo_r.at[3], to_d(before)),
    ]
    arrive(halo)
    hg[mine, 0:LAYER] = jnp.where(d == 0, 0.0, hl2[0].astype(F32)).astype(BF)
    hg[mine, LAYER : 2 * LAYER] = jnp.where(d == 63, 0.0, hl2[1].astype(F32)).astype(BF)
    got_halo = exchange(13, y, to_y, lambda p: hg.at[mine, :], hg.at[mine, :])
    arrive(got)

    vs[0:432, :] = nt(s9c[...], glw[...])

    def rows64(b):
        return pl.ds(pl.multiple_of(b * 64, 64), 64)

    def rows256(b):
        return pl.ds(pl.multiple_of(b * 256, 256), 256)

    def grad_expand(i, carry):
        expand(glw, gx, i)
        return carry

    def input_step(i, carry):
        total = None
        for dx in range(3):
            field = gx[:, span(i, (2 - dx) * LAYER)]
            term = nn(wb_ref[dx * 144 : dx * 144 + 144, :], field)
            total = term if total is None else total + term
        conv = jnp.zeros((16, 512), F32)
        for j, (dy, dz) in enumerate(taps):
            shift = (dy * 16 + dz) % 512
            slab = total[j * 16 : j * 16 + 16]
            slab = pltpu.roll(slab, shift, 1) if shift else slab
            conv = conv + jnp.where(in_layer(512, -dy, -dz), slab, 0.0)
        own_grad = gx[mine, span(i, LAYER)].astype(F32)
        gf_ref[:, span(i)] = own_grad + jnp.where(ss_ref[:, span(i)] >= 0, conv, 0.0)
        return carry

    def pair_send(src, dst, n):
        return send(src, dst, red_s.at[n], red_r.at[n], {"vox_2": 1 - core})

    def x_send(src_of, dst, n):
        copies = []
        for r in (2, 1, 3):
            p = lax.rem(x + r, 4)
            copies.append(send(src_of(p), dst, red_s.at[n + r], red_r.at[n + r], to_x(p)))
        return copies

    got = [pair_send(vs.at[rows256(1 - core), :], half, 0)]
    arrive(got)
    pair[...] = vs[rows256(core), :] + half[...]
    quad[x] = pair[rows64(x), :]
    got = x_send(lambda p: pair.at[rows64(p), :], quad.at[x], 0)
    drain()
    lax.fori_loop(0, 8, grad_expand, 0)
    arrive(got)
    own64[...] = (quad[0] + quad[1] + quad[2] + quad[3]).astype(BF)
    zsrc[z] = own64[...]
    got = exchange(14, z, to_z, lambda p: own64, zsrc.at[z])
    drain()
    arrive(got_halo)
    gx[:, 0:LAYER] = hg[:, 0:LAYER]
    gx[:, LAYER + CELLS : EXT] = hg[:, LAYER : 2 * LAYER]
    lax.fori_loop(0, 6, input_step, 0)
    arrive(got)
    total = zsrc[0].astype(F32)
    for i in range(1, 8):
        total = total + zsrc[i].astype(F32)
    zall[...] = total
    back256[rows64(x), :] = total
    got = x_send(lambda p: zall, back256.at[rows64(x), :], 4)
    lax.fori_loop(6, 8, input_step, 0)
    stores[1].start()
    arrive(got)
    got = [pair_send(back256, back64, 8)]
    vv_ref[rows256(core), :] = back256[...]
    drain()
    arrive(got)
    vv_ref[rows256(1 - core), :] = back64[...]
    stores[2].start()
    drain()
    drain()
    for store in stores:
        store.wait()


def store_kernel(
    bo_ref, gf_ref, vv_ref, bo_out, gf_out, gc_out, gq_out, go_out, bo, gf, vv, in_sem, out_sem
):
    loads = [
        pltpu.make_async_copy(src, dst, in_sem.at[i])
        for i, (src, dst) in enumerate(((gf_ref, gf), (vv_ref, vv), (bo_ref, bo)))
    ]
    stores = [
        pltpu.make_async_copy(src, dst, out_sem.at[i])
        for i, (src, dst) in enumerate(
            (
                (gf, gf_out), (vv.at[0:432, :], gc_out), (vv.at[432:480, :], gq_out),
                (vv.at[480:496, :], go_out), (bo, bo_out),
            )
        )
    ]
    for load in loads:
        load.start()
    for load, behind in zip(loads, (stores[0:1], stores[1:4], stores[4:5])):
        load.wait()
        for store in behind:
            store.start()
    for store in stores:
        store.wait()


def body(
    features, conv_weight, qkv_weight, out_weight, cotangent, neighbours, send_slot, recv_slot
):
    wb = jnp.transpose(conv_weight, (0, 2, 1)).reshape(432, 128)
    w2 = jnp.transpose(qkv_weight, (0, 2, 1)).reshape(48, 128)

    def buf(*shape):
        return pltpu.VMEM(shape, BF)

    def wide(*shape):
        return pltpu.VMEM(shape, F32)

    scratch = [
        buf(16, SLOTS), wide(16, CELLS), wide(512, 128),
        buf(16, CELLS), pltpu.VMEM((1, CELLS), jnp.int32), pltpu.VMEM((1, SLOTS), jnp.int32),
        buf(16, SLOTS), buf(432, 128), buf(48, 128), buf(16, 128),
        buf(SLOTS, CELLS), buf(SLOTS, SLOTS),
        buf(128, EXT), buf(128, 512), buf(2, 16, LAYER), buf(16, CELLS),
        buf(128, SLOTS), buf(128, 512), buf(8, 16, 512), buf(432, 128),
        buf(432, 20 * LAYER), buf(432, SLOTS), buf(16, CELLS), wide(16, SLOTS),
        buf(8, 16, 128), buf(8, 16, 128), buf(8, 16, 128), buf(8, 16, 128),
        buf(128, SLOTS), buf(128, SLOTS), buf(64, 128), buf(8, 64, 128),
        buf(SLOTS, 128), buf(128, SLOTS), buf(128, SLOTS), buf(48, SLOTS),
        buf(16, SLOTS), wide(SLOTS, 256), buf(SLOTS, 256), buf(SLOTS, 256),
        buf(64, SLOTS), wide(32, SLOTS), buf(128, SLOTS),
        buf(8, 32, 128), buf(8, 64, 128), buf(8, 32, 128),
        buf(8, 16, 128), buf(8, 16, 128), buf(8, 16, 128),
        buf(128, SLOTS), buf(128, EXT), buf(16, 512), buf(2, 16, LAYER), buf(128, 512),
        wide(512, 128), buf(8, 16, 128), wide(256, 128), wide(256, 128),
        wide(4, 64, 128), buf(64, 128), buf(8, 64, 128), wide(64, 128),
        wide(256, 128), wide(256, 128),
        pltpu.SemaphoreType.DMA((7,)), pltpu.SemaphoreType.DMA((3,)),
        pltpu.SemaphoreType.DMA((15, 8)), pltpu.SemaphoreType.DMA((15, 8)),
        pltpu.SemaphoreType.DMA((4,)), pltpu.SemaphoreType.DMA((4,)),
        pltpu.SemaphoreType.DMA((9,)), pltpu.SemaphoreType.DMA((9,)),
    ]
    hbm = pl.BlockSpec(memory_space=pltpu.HBM)
    block_out, grad_features, sums = pl.pallas_call(
        whole_kernel,
        out_shape=(
            jax.ShapeDtypeStruct((16, SLOTS), BF),
            jax.ShapeDtypeStruct((16, CELLS), F32),
            jax.ShapeDtypeStruct((512, 128), F32),
        ),
        in_specs=[hbm] * 7,
        out_specs=(hbm, hbm, hbm),
        scratch_shapes=scratch,
        compiler_params=pltpu.CompilerParams(
            collective_id=0, has_side_effects=True, vmem_limit_bytes=67043328
        ),
    )(
        features, send_slot.reshape(1, CELLS), recv_slot.reshape(1, SLOTS), cotangent,
        wb, w2, out_weight,
    )
    block_out, grad_features, grad_conv, grad_qkv, grad_out = pl.pallas_call(
        store_kernel,
        out_shape=(
            jax.ShapeDtypeStruct((16, SLOTS), BF),
            jax.ShapeDtypeStruct((16, CELLS), F32),
            jax.ShapeDtypeStruct((432, 128), F32),
            jax.ShapeDtypeStruct((48, 128), F32),
            jax.ShapeDtypeStruct((16, 128), F32),
        ),
        in_specs=[hbm] * 3,
        out_specs=(hbm,) * 5,
        scratch_shapes=[
            buf(16, SLOTS), wide(16, CELLS), wide(512, 128),
            pltpu.SemaphoreType.DMA((3,)), pltpu.SemaphoreType.DMA((5,)),
        ],
        compiler_params=pltpu.CompilerParams(vmem_limit_bytes=67043328),
    )(block_out, grad_features, sums)
    grad_conv = jnp.transpose(grad_conv.reshape(27, 16, 128), (0, 2, 1))
    grad_qkv = jnp.transpose(grad_qkv.reshape(3, 16, 128), (0, 2, 1))
    return (block_out, grad_features, grad_conv, grad_qkv, grad_out)


def solution(mesh):
    torus = Mesh(mesh.devices.reshape(8, 4, 2, mesh.shape["ch"]), ("vox_0", "vox_1", "vox_2", "ch"))
    placed = (
        P("ch", VOX),
        P(None, None, "ch"),
        P(None, None, "ch"),
        P("ch", None),
        P("ch", VOX),
        P(None, VOX),
        P(VOX),
        P(VOX),
    )
    return jax.shard_map(
        body,
        mesh=torus,
        in_specs=placed,
        out_specs=(
            P("ch", VOX),
            P("ch", VOX),
            P(None, None, "ch"),
            P(None, None, "ch"),
            P("ch", None),
        ),
        check_vma=False,
    )
```

```python
import jax
import jax.numpy as jnp
from jax import lax
from jax.experimental import pallas as pl
from jax.experimental.pallas import tpu as pltpu
from jax.sharding import Mesh
from jax.sharding import PartitionSpec as P

MESH = pl.DeviceIdType.MESH
VOX = ("vox_0", "vox_1", "vox_2")
BF = jnp.bfloat16
F32 = jnp.float32
CELLS = 4096
LAYER = 256
EXT = CELLS + 2 * LAYER
SLOTS = 1024
ORDER = (4, 3, 5, 2, 6, 1, 7)


def nn(a, b):
    return jnp.dot(a, b, preferred_element_type=F32)


def nt(a, b):
    return lax.dot_general(a, b, (((1,), (1,)), ((), ())), preferred_element_type=F32)


def tn(a, b):
    return lax.dot_general(a, b, (((0,), (0,)), ((), ())), preferred_element_type=F32)


def lanes(shape):
    return lax.broadcasted_iota(jnp.int32, shape, 1)


def swap_blocks(tiles):
    flat = tiles.reshape(128, 128)
    turned = [flat if s == 0 else pltpu.roll(flat, s * 16, 1) for s in range(8)]
    block = lanes((16, 128)) // 16
    out = []
    for j in range(8):
        tile = turned[(0 - j) % 8][0:16]
        for i in range(1, 8):
            tile = jnp.where(block == i, turned[(i - j) % 8][i * 16 : i * 16 + 16], tile)
        out.append(tile)
    return out


def in_layer(width, dy, dz):
    cell = lanes((16, width))
    row = (cell // 16) % 16 + dy
    col = cell % 16 + dz
    return (row >= 0) & (row < 16) & (col >= 0) & (col < 16)


def whole_kernel(
    f_in, ss_in, rs_in, cot_in, wb_in, w2_in, ow_in,
    bo_out, gf_out, vv_out,
    bo_ref, gf_ref, vv_ref, f_ref, ss_ref, rs_ref, cot_ref, wb_ref, w2_ref, ow_ref,
    onehot, pick, fx, hx, hl, fm, fc, wt, aw, w9, s27, s9c, layer, s1acc,
    s1, a1, t1, a2, gw, cw, mine2, ww,
    kvt, qq, gg, qkv, gaw, lg, pr, sc, pk, acc, big, xs, ys, u1, c2, v1, d1,
    glw, gx, hf, hl2, hg, vs, e0, half, pair, quad, own64, zsrc, zall, back64, back256,
    in_sem, out_sem, ex_s, ex_r, halo_s, halo_r, red_s, red_r,
):
    z = lax.axis_index("vox_0")
    x = lax.axis_index("vox_1")
    core = lax.axis_index("vox_2")
    xc = x * 2 + core
    y = lax.axis_index("ch")
    d = z * 8 + xc

    def to_y(p):
        return {"ch": p}

    def to_z(p):
        return {"vox_0": p}

    def to_x(p):
        return {"vox_1": p}

    def to_xc(p):
        return {"vox_1": p // 2, "vox_2": lax.rem(p, 2)}

    def to_d(p):
        return {"vox_0": p // 8, "vox_1": lax.rem(p, 8) // 2, "vox_2": lax.rem(p, 2)}

    after, before = lax.rem(d + 1, 64), lax.rem(d + 63, 64)

    barrier = pltpu.get_barrier_semaphore()
    for r in range(1, 8):
        for me, where in ((y, to_y), (z, to_z), (xc, to_xc)):
            pl.semaphore_signal(
                barrier, inc=1, device_id=where(lax.rem(me + r, 8)), device_id_type=MESH
            )
    for p in (after, before):
        pl.semaphore_signal(barrier, inc=1, device_id=to_d(p), device_id_type=MESH)

    loads = [
        pltpu.make_async_copy(src, dst, in_sem.at[i])
        for i, (src, dst) in enumerate(
            (
                (ss_in, ss_ref), (f_in, f_ref), (wb_in, wb_ref), (rs_in, rs_ref),
                (cot_in, cot_ref), (w2_in, w2_ref), (ow_in, ow_ref),
            )
        )
    ]
    for load in loads:
        load.start()

    fresh, old = [], []

    def send(src, dst, s_sem, r_sem, where):
        copy = pltpu.make_async_remote_copy(
            src_ref=src, dst_ref=dst, send_sem=s_sem, recv_sem=r_sem,
            device_id=where, device_id_type=MESH,
        )
        copy.start()
        fresh.append(copy)
        return copy

    def drain():
        for copy in old:
            copy.wait_send()
        old[:] = fresh
        fresh.clear()

    def exchange(phase, me, where, src_of, dst):
        copies = []
        for r in ORDER:
            p = lax.rem(me + r, 8)
            copies.append(
                send(src_of(p), dst, ex_s.at[phase, r], ex_r.at[phase, r], where(p))
            )
        return copies

    def arrive(copies):
        for copy in copies:
            copy.wait_recv()

    def rows16(b):
        return pl.ds(pl.multiple_of(b * 16, 16), 16)

    def tile(b):
        return pl.ds(pl.multiple_of(b * 128, 128), 128)

    def span(i, start=0, size=512):
        return pl.ds(pl.multiple_of(i * 512 + start, 256), size)

    mine = rows16(y)
    loads[0].wait()

    def onehot_step(i, carry):
        at = pl.multiple_of(i * 16, 16)
        ids = lax.broadcasted_iota(jnp.int32, (16, CELLS), 0) + at
        onehot[pl.ds(at, 16), :] = jnp.where(ids == ss_ref[...], 1.0, 0.0).astype(BF)
        return carry

    lax.fori_loop(0, 64, onehot_step, 0)

    loads[1].wait()
    fm[...] = jnp.where(ss_ref[...] >= 0, f_ref[...].astype(F32), 0.0).astype(BF)

    loads[2].wait()
    weights = jnp.concatenate([wb_ref[...].astype(F32), jnp.zeros((80, 128), F32)], axis=0)
    for t in range(4):
        wt[:, t * 128 : t * 128 + 128] = weights[t * 128 : t * 128 + 128, :].T.astype(BF)

    pl.semaphore_wait(barrier, 23)
    halo = [
        send(fm.at[:, CELLS - LAYER : CELLS], hl.at[0], halo_s.at[0], halo_r.at[0], to_d(after)),
        send(fm.at[:, 0:LAYER], hl.at[1], halo_s.at[1], halo_r.at[1], to_d(before)),
    ]
    got_aw = exchange(11, y, to_y, lambda p: wt.at[rows16(p), :], aw.at[y])
    def compact_step(i, carry):
        at = pl.multiple_of(i * 256, 256)
        fc[mine, pl.ds(at, 256)] = nt(fm[...], onehot[pl.ds(at, 256), :]).astype(BF)
        return carry

    lax.fori_loop(0, 4, compact_step, 0)

    got = exchange(0, y, to_y, lambda p: fc.at[mine, :], fc.at[mine, :])

    aw[y] = wt[mine, :]
    for load in loads[3:]:
        load.wait()
    live = rs_ref[...] >= 0
    cw[mine, :] = jnp.where(live, cot_ref[...].astype(F32), 0.0).astype(BF)
    mine2[0:48, :] = w2_ref[...]
    mine2[48:64, :] = ow_ref[...]
    ww[y] = mine2[...]
    source = rs_ref[...]
    route = (source >> 4) & 7
    spot = jnp.where(live, route * 128 + ((source >> 7) & 7) * 16 + (source & 15), -1)

    arrive(halo)
    hx[mine, 0:LAYER] = jnp.where(d == 0, 0.0, hl[0].astype(F32)).astype(BF)
    hx[mine, LAYER : 2 * LAYER] = jnp.where(d == 63, 0.0, hl[1].astype(F32)).astype(BF)
    got_hx = exchange(12, y, to_y, lambda p: hx.at[mine, :], hx.at[mine, :])

    taps = [(dy, dz) for dy in (-1, 0, 1) for dz in (-1, 0, 1)]

    def shifted(values, width, put):
        for j, (dy, dz) in enumerate(taps):
            shift = -(dy * 16 + dz) % width
            slab = pltpu.roll(values, shift, 1) if shift else values
            slab = jnp.where(in_layer(width, dy, dz), slab, 0.0).astype(BF)
            for dx in range(3):
                put(dx, dx * 144 + j * 16, slab)

    def shifted_step(i, carry):
        def put(dx, row, slab):
            s27[row : row + 16, span(i, (3 - dx) * LAYER)] = slab

        shifted(fm[:, span(i)].astype(F32), 512, put)
        return carry

    lax.fori_loop(0, 8, shifted_step, 0)
    edges = hx[mine, :].astype(F32)

    def put_left(dx, row, slab):
        s27[row : row + 16, (2 - dx) * LAYER : (3 - dx) * LAYER] = slab[:, 0:LAYER]

    def put_right(dx, row, slab):
        s27[row : row + 16, (19 - dx) * LAYER : (20 - dx) * LAYER] = slab[:, LAYER : 2 * LAYER]

    shifted(edges, 512, put_left)
    shifted(edges, 512, put_right)

    def s9c_step(i, carry):
        at = pl.multiple_of(i * 256, 256)
        s9c[:, pl.ds(at, 256)] = nt(
            s27[:, 512 : 512 + CELLS], onehot[pl.ds(at, 256), :]
        ).astype(BF)
        return carry

    def pick_step(i, carry):
        at = pl.multiple_of(i * 16, 16)
        ids = lax.broadcasted_iota(jnp.int32, (16, SLOTS), 0) + at
        pick[pl.ds(at, 16), :] = jnp.where(ids == spot, 1.0, 0.0).astype(BF)
        return carry

    qq[...] = jnp.zeros((128, SLOTS), BF)
    gg[...] = jnp.zeros((128, SLOTS), BF)
    s1acc[...] = jnp.zeros((16, SLOTS), F32)
    acc[...] = jnp.zeros((32, SLOTS), F32)

    arrive(got_aw)
    for t in range(4):
        for k, part in enumerate(swap_blocks(aw[:, :, t * 128 : t * 128 + 128].astype(F32))):
            if t * 8 + k < 27:
                at = (t * 8 + k) * 16
                w9[at : at + 16, :] = part.astype(BF)

    arrive(got)
    got_ww = exchange(1, y, to_y, lambda p: mine2, ww.at[y])
    got_cw = exchange(2, y, to_y, lambda p: cw.at[mine, :], cw.at[mine, :])
    drain()

    def expand(src, dst, i):
        dst[:, span(i, LAYER)] = nn(src[...], onehot[:, span(i)]).astype(BF)

    def conv(i):
        total = None
        for dx in range(3):
            field = fx[:, span(i, dx * LAYER)]
            term = nn(w9[dx * 144 : dx * 144 + 144, :], field)
            total = term if total is None else total + term
        out = fm[:, span(i)].astype(F32)
        summed = jnp.zeros((16, 512), F32)
        for j, (dy, dz) in enumerate(taps):
            shift = -(dy * 16 + dz) % 512
            slab = total[j * 16 : j * 16 + 16]
            slab = pltpu.roll(slab, shift, 1) if shift else slab
            summed = summed + jnp.where(in_layer(512, dy, dz), slab, 0.0)
        layer[:, span(i)] = (out + summed).astype(BF)

    def pack(i):
        s1acc[...] += nt(layer[:, span(i)], onehot[:, span(i)])

    for i in range(4):
        expand(fc, fx, i)
    conv(1)

    def conv_step(i, carry):
        pack(i - 1)
        conv(i)
        expand(fc, fx, i + 2)
        return carry

    lax.fori_loop(2, 6, conv_step, 0)
    pack(5)
    conv(6)
    pack(6)
    arrive(got_hx)
    fx[:, 0:LAYER] = hx[:, 0:LAYER]
    fx[:, LAYER + CELLS : EXT] = hx[:, LAYER : 2 * LAYER]
    conv(0)
    pack(0)
    conv(7)
    pack(7)
    packed = s1acc[...].astype(BF)
    for t in range(8):
        s1[t] = packed[:, t * 128 : t * 128 + 128]
    a1[z] = s1[z]
    got = exchange(3, z, to_z, lambda p: s1.at[p], a1.at[z])
    lax.fori_loop(0, 64, pick_step, 0)
    lax.fori_loop(0, 2, s9c_step, 0)

    drain()
    arrive(got)
    for j, part in enumerate(swap_blocks(a1[...].astype(F32))):
        t1[j] = part.astype(BF)
    a2[xc] = t1[xc]
    got = exchange(4, xc, to_xc, lambda p: t1.at[p], a2.at[xc])
    drain()
    arrive(got)
    arrived = jnp.concatenate([a2[i] for i in range(8)], axis=1)
    gw[mine, :] = nn(arrived, pick[...]).astype(BF)
    got = exchange(5, y, to_y, lambda p: gw.at[mine, :], gw.at[mine, :])
    drain()
    arrive(got_cw)
    arrive(got_ww)
    ga = nn(ow_ref[...], cw[...]).astype(BF)
    gaw[...] = ga
    gg[32:48, :] = (ga.astype(F32) * 0.25).astype(BF)
    lax.fori_loop(2, 4, s9c_step, 0)
    arrive(got)

    whole = gw[...].astype(F32)
    mean = jnp.mean(whole, axis=0, keepdims=True)
    centred = whole - mean
    var = jnp.mean(centred * centred, axis=0, keepdims=True)
    normed = (centred * lax.rsqrt(var + 1e-05)).astype(BF)
    big[...] = normed
    rows = nn(w2_ref[...], normed).astype(BF)
    qkv[...] = rows
    qq[0:16, :] = (rows[0:16].astype(F32) * 0.25).astype(BF)
    row = lax.broadcasted_iota(jnp.int32, (16, SLOTS), 0)
    qq[16:32, :] = jnp.where(row == 0, 1.0, 0.0).astype(BF)
    bias = jnp.where((row == 0) & (~live), -1e30, 0.0)
    stacked = jnp.concatenate(
        [
            rows[16:32].astype(F32),
            bias,
            rows[32:48].astype(F32),
            jnp.zeros((80, SLOTS), F32),
        ],
        axis=0,
    )
    for t in range(8):
        kvt[t * 128 : t * 128 + 128, :] = stacked[:, t * 128 : t * 128 + 128].T.astype(BF)

    def attend_step(i, carry):
        at = pl.ds(pl.multiple_of(i * 256, 256), 256)
        top = None
        for c in range(4):
            cells = slice(c * 256, c * 256 + 256)
            logits = nn(kvt[cells, :], qq[:, at])
            lg[cells, :] = logits
            most = jnp.max(logits.reshape(32, 8, 256), axis=0)
            top = most if top is None else jnp.maximum(top, most)
        top = jnp.max(top, axis=0, keepdims=True)
        total = jnp.zeros((8, 256), F32)
        for c in range(16):
            cells = slice(c * 64, c * 64 + 64)
            exponents = jnp.exp(lg[cells, :] - top)
            lg[cells, :] = exponents
            total = total + jnp.sum(exponents.reshape(8, 8, 256), axis=0)
        inverse_total = 1.0 / jnp.sum(total, axis=0, keepdims=True)
        for c in range(16):
            cells = slice(c * 64, c * 64 + 64)
            pr[cells, :] = (lg[cells, :] * inverse_total).astype(BF)
        attended = nn(qkv[32:48, :], pr[...])
        pk[0:16, at] = attended.astype(BF)
        inner = jnp.sum(attended * gg[32:48, at].astype(F32), axis=0, keepdims=True)
        acc[16:32, :] += nt(gaw[:, at], pr[...])
        for c in range(4):
            cells = slice(c * 256, c * 256 + 256)
            grad_logits = nn(kvt[cells, :], gg[:, at])
            sc[cells, :] = (pr[cells, :].astype(F32) * (grad_logits - inner)).astype(BF)
        pk[16:32, at] = nn(qkv[16:32, :], sc[...]).astype(BF)
        acc[0:16, :] += nt(qkv[0:16, at], sc[...])
        return carry

    lax.fori_loop(0, 4, attend_step, 0)
    pk[32:64, :] = acc[...].astype(BF)

    ys[y] = pk[:, tile(y)]
    got = exchange(6, y, to_y, lambda p: pk.at[:, tile(p)], ys.at[y])
    drain()
    vs[432:480, :] = nt(pk[16:64, :], big[...])
    vs[480:496, :] = nt(pk[0:16, :], cw[...])
    vs[496:512, :] = jnp.zeros((16, 128), F32)
    own_slots = tile(y)
    part = gw[:, own_slots].astype(F32)
    mean = jnp.mean(part, axis=0, keepdims=True)
    centred = part - mean
    var = jnp.mean(centred * centred, axis=0, keepdims=True)
    inverse = lax.rsqrt(var + 1e-05)
    normal = centred * inverse
    cot = cw[:, own_slots].astype(F32)
    live_part = rs_ref[:, own_slots] >= 0
    arrive(got)
    mixed = tn(ww[:, 48:64, :].reshape(128, 128), ys[:, 0:16, :].reshape(128, 128))
    grad = None
    for i in range(3):
        term = tn(
            ww[:, i * 16 : i * 16 + 16, :].reshape(128, 128),
            ys[:, 16 + i * 16 : 32 + i * 16, :].reshape(128, 128),
        )
        grad = term if grad is None else grad + term
    grad = grad.astype(BF).astype(F32)
    grad_ln = inverse * (
        grad
        - jnp.mean(grad, axis=0, keepdims=True)
        - normal * jnp.mean(grad * normal, axis=0, keepdims=True)
    )
    back = jnp.where(live_part, cot + grad_ln, 0.0).astype(BF)
    block = jnp.where(live_part, part + mixed, 0.0).astype(BF)
    xs[:, 0:16, :] = back.reshape(8, 16, 128)
    xs[:, 16:32, :] = block.reshape(8, 16, 128)
    u1[y] = xs[y]
    got = exchange(7, y, to_y, lambda p: xs.at[p], u1.at[y])
    drain()
    arrive(got)
    grad_grouped = jnp.concatenate([u1[i, 0:16] for i in range(8)], axis=1)
    spread = nt(grad_grouped, pick[...])
    for t in range(8):
        c2[t] = spread[:, t * 128 : t * 128 + 128].astype(BF)
    v1[xc] = c2[xc]
    got = exchange(8, xc, to_xc, lambda p: c2.at[p], v1.at[xc])
    drain()
    bo_ref[...] = jnp.concatenate([u1[i, 16:32] for i in range(8)], axis=1)
    stores = [
        pltpu.make_async_copy(src, dst, out_sem.at[i])
        for i, (src, dst) in enumerate(((bo_ref, bo_out), (gf_ref, gf_out), (vv_ref, vv_out)))
    ]
    stores[0].start()
    arrive(got)
    for j, piece in enumerate(swap_blocks(v1[...].astype(F32))):
        d1[j] = piece.astype(BF)
    e0[z] = d1[z]
    got = exchange(9, z, to_z, lambda p: d1.at[p], e0.at[z])
    drain()
    arrive(got)
    slots = jnp.concatenate([e0[i] for i in range(8)], axis=1)
    glw[mine, :] = slots
    got = exchange(10, y, to_y, lambda p: glw.at[mine, :], glw.at[mine, :])
    drain()
    hf[:, 0:LAYER] = nn(slots, onehot[:, 0:LAYER]).astype(BF)
    hf[:, LAYER : 2 * LAYER] = nn(slots, onehot[:, CELLS - LAYER : CELLS]).astype(BF)
    halo = [
        send(hf.at[:, LAYER : 2 * LAYER], hl2.at[0], halo_s.at[2], halo_r.at[2], to_d(after)),
        send(hf.at[:, 0:LAYER], hl2.at[1], halo_s.at[3], halo_r.at[3], to_d(before)),
    ]
    arrive(halo)
    hg[mine, 0:LAYER] = jnp.where(d == 0, 0.0, hl2[0].astype(F32)).astype(BF)
    hg[mine, LAYER : 2 * LAYER] = jnp.where(d == 63, 0.0, hl2[1].astype(F32)).astype(BF)
    got_halo = exchange(13, y, to_y, lambda p: hg.at[mine, :], hg.at[mine, :])
    arrive(got)

    vs[0:432, :] = nt(s9c[...], glw[...])

    def rows64(b):
        return pl.ds(pl.multiple_of(b * 64, 64), 64)

    def rows256(b):
        return pl.ds(pl.multiple_of(b * 256, 256), 256)

    def grad_expand(i, carry):
        expand(glw, gx, i)
        return carry

    def input_step(i, carry):
        total = None
        for dx in range(3):
            field = gx[:, span(i, (2 - dx) * LAYER)]
            term = nn(wb_ref[dx * 144 : dx * 144 + 144, :], field)
            total = term if total is None else total + term
        conv = jnp.zeros((16, 512), F32)
        for j, (dy, dz) in enumerate(taps):
            shift = (dy * 16 + dz) % 512
            slab = total[j * 16 : j * 16 + 16]
            slab = pltpu.roll(slab, shift, 1) if shift else slab
            conv = conv + jnp.where(in_layer(512, -dy, -dz), slab, 0.0)
        own_grad = gx[mine, span(i, LAYER)].astype(F32)
        gf_ref[:, span(i)] = own_grad + jnp.where(ss_ref[:, span(i)] >= 0, conv, 0.0)
        return carry

    def pair_send(src, dst, n):
        return send(src, dst, red_s.at[n], red_r.at[n], {"vox_2": 1 - core})

    def x_send(src_of, dst, n):
        copies = []
        for r in (2, 1, 3):
            p = lax.rem(x + r, 4)
            copies.append(send(src_of(p), dst, red_s.at[n + r], red_r.at[n + r], to_x(p)))
        return copies

    got = [pair_send(vs.at[rows256(1 - core), :], half, 0)]
    arrive(got)
    pair[...] = vs[rows256(core), :] + half[...]
    quad[x] = pair[rows64(x), :]
    got = x_send(lambda p: pair.at[rows64(p), :], quad.at[x], 0)
    drain()
    lax.fori_loop(0, 8, grad_expand, 0)
    arrive(got)
    own64[...] = (quad[0] + quad[1] + quad[2] + quad[3]).astype(BF)
    zsrc[z] = own64[...]
    got = exchange(14, z, to_z, lambda p: own64, zsrc.at[z])
    drain()
    arrive(got_halo)
    gx[:, 0:LAYER] = hg[:, 0:LAYER]
    gx[:, LAYER + CELLS : EXT] = hg[:, LAYER : 2 * LAYER]
    lax.fori_loop(0, 6, input_step, 0)
    arrive(got)
    total = zsrc[0].astype(F32)
    for i in range(1, 8):
        total = total + zsrc[i].astype(F32)
    zall[...] = total
    back256[rows64(x), :] = total
    got = x_send(lambda p: zall, back256.at[rows64(x), :], 4)
    lax.fori_loop(6, 8, input_step, 0)
    stores[1].start()
    arrive(got)
    got = [pair_send(back256, back64, 8)]
    vv_ref[rows256(core), :] = back256[...]
    drain()
    arrive(got)
    vv_ref[rows256(1 - core), :] = back64[...]
    stores[2].start()
    drain()
    drain()
    for store in stores:
        store.wait()


def store_kernel(
    bo_ref, gf_ref, vv_ref, bo_out, gf_out, gc_out, gq_out, go_out, bo, gf, vv, in_sem, out_sem
):
    loads = [
        pltpu.make_async_copy(src, dst, in_sem.at[i])
        for i, (src, dst) in enumerate(((gf_ref, gf), (vv_ref, vv), (bo_ref, bo)))
    ]
    stores = [
        pltpu.make_async_copy(src, dst, out_sem.at[i])
        for i, (src, dst) in enumerate(
            (
                (gf, gf_out), (vv.at[0:432, :], gc_out), (vv.at[432:480, :], gq_out),
                (vv.at[480:496, :], go_out), (bo, bo_out),
            )
        )
    ]
    for load in loads:
        load.start()
    for load, behind in zip(loads, (stores[0:1], stores[1:4], stores[4:5])):
        load.wait()
        for store in behind:
            store.start()
    for store in stores:
        store.wait()


def body(
    features, conv_weight, qkv_weight, out_weight, cotangent, neighbours, send_slot, recv_slot
):
    wb = jnp.transpose(conv_weight, (0, 2, 1)).reshape(432, 128)
    w2 = jnp.transpose(qkv_weight, (0, 2, 1)).reshape(48, 128)

    def buf(*shape):
        return pltpu.VMEM(shape, BF)

    def wide(*shape):
        return pltpu.VMEM(shape, F32)

    scratch = [
        buf(16, SLOTS), wide(16, CELLS), wide(512, 128),
        buf(16, CELLS), pltpu.VMEM((1, CELLS), jnp.int32), pltpu.VMEM((1, SLOTS), jnp.int32),
        buf(16, SLOTS), buf(432, 128), buf(48, 128), buf(16, 128),
        buf(SLOTS, CELLS), buf(SLOTS, SLOTS),
        buf(128, EXT), buf(128, 512), buf(2, 16, LAYER), buf(16, CELLS),
        buf(128, SLOTS), buf(128, 512), buf(8, 16, 512), buf(432, 128),
        buf(432, 20 * LAYER), buf(432, SLOTS), buf(16, CELLS), wide(16, SLOTS),
        buf(8, 16, 128), buf(8, 16, 128), buf(8, 16, 128), buf(8, 16, 128),
        buf(128, SLOTS), buf(128, SLOTS), buf(64, 128), buf(8, 64, 128),
        buf(SLOTS, 128), buf(128, SLOTS), buf(128, SLOTS), buf(48, SLOTS),
        buf(16, SLOTS), wide(SLOTS, 256), buf(SLOTS, 256), buf(SLOTS, 256),
        buf(64, SLOTS), wide(32, SLOTS), buf(128, SLOTS),
        buf(8, 32, 128), buf(8, 64, 128), buf(8, 32, 128),
        buf(8, 16, 128), buf(8, 16, 128), buf(8, 16, 128),
        buf(128, SLOTS), buf(128, EXT), buf(16, 512), buf(2, 16, LAYER), buf(128, 512),
        wide(512, 128), buf(8, 16, 128), wide(256, 128), wide(256, 128),
        wide(4, 64, 128), buf(64, 128), buf(8, 64, 128), wide(64, 128),
        wide(256, 128), wide(256, 128),
        pltpu.SemaphoreType.DMA((7,)), pltpu.SemaphoreType.DMA((3,)),
        pltpu.SemaphoreType.DMA((15, 8)), pltpu.SemaphoreType.DMA((15, 8)),
        pltpu.SemaphoreType.DMA((4,)), pltpu.SemaphoreType.DMA((4,)),
        pltpu.SemaphoreType.DMA((9,)), pltpu.SemaphoreType.DMA((9,)),
    ]
    hbm = pl.BlockSpec(memory_space=pltpu.HBM)
    block_out, grad_features, sums = pl.pallas_call(
        whole_kernel,
        out_shape=(
            jax.ShapeDtypeStruct((16, SLOTS), BF),
            jax.ShapeDtypeStruct((16, CELLS), F32),
            jax.ShapeDtypeStruct((512, 128), F32),
        ),
        in_specs=[hbm] * 7,
        out_specs=(hbm, hbm, hbm),
        scratch_shapes=scratch,
        compiler_params=pltpu.CompilerParams(
            collective_id=0, has_side_effects=True, vmem_limit_bytes=67043328
        ),
    )(
        features, send_slot.reshape(1, CELLS), recv_slot.reshape(1, SLOTS), cotangent,
        wb, w2, out_weight,
    )
    block_out, grad_features, grad_conv, grad_qkv, grad_out = pl.pallas_call(
        store_kernel,
        out_shape=(
            jax.ShapeDtypeStruct((16, SLOTS), BF),
            jax.ShapeDtypeStruct((16, CELLS), F32),
            jax.ShapeDtypeStruct((432, 128), F32),
            jax.ShapeDtypeStruct((48, 128), F32),
            jax.ShapeDtypeStruct((16, 128), F32),
        ),
        in_specs=[hbm] * 3,
        out_specs=(hbm,) * 5,
        scratch_shapes=[
            buf(16, SLOTS), wide(16, CELLS), wide(512, 128),
            pltpu.SemaphoreType.DMA((3,)), pltpu.SemaphoreType.DMA((5,)),
        ],
        compiler_params=pltpu.CompilerParams(vmem_limit_bytes=67043328),
    )(block_out, grad_features, sums)
    grad_conv = jnp.transpose(grad_conv.reshape(27, 16, 128), (0, 2, 1))
    grad_qkv = jnp.transpose(grad_qkv.reshape(3, 16, 128), (0, 2, 1))
    return (block_out, grad_features, grad_conv, grad_qkv, grad_out)


def solution(mesh):
    torus = Mesh(mesh.devices.reshape(8, 4, 2, mesh.shape["ch"]), ("vox_0", "vox_1", "vox_2", "ch"))
    placed = (
        P("ch", VOX),
        P(None, None, "ch"),
        P(None, None, "ch"),
        P("ch", None),
        P("ch", VOX),
        P(None, VOX),
        P(VOX),
        P(VOX),
    )
    return jax.shard_map(
        body,
        mesh=torus,
        in_specs=placed,
        out_specs=(
            P("ch", VOX),
            P("ch", VOX),
            P(None, None, "ch"),
            P(None, None, "ch"),
            P("ch", None),
        ),
        check_vma=False,
    )
```

```python
import jax
import jax.numpy as jnp
from jax import lax
from jax.experimental import pallas as pl
from jax.experimental.pallas import tpu as pltpu
from jax.sharding import Mesh
from jax.sharding import PartitionSpec as P

MESH = pl.DeviceIdType.MESH
VOX = ("vox_0", "vox_1", "vox_2")
BF = jnp.bfloat16
F32 = jnp.float32
CELLS = 4096
LAYER = 256
EXT = CELLS + 2 * LAYER
SLOTS = 1024
ORDER = (4, 3, 5, 2, 6, 1, 7)


def nn(a, b):
    return jnp.dot(a, b, preferred_element_type=F32)


def nt(a, b):
    return lax.dot_general(a, b, (((1,), (1,)), ((), ())), preferred_element_type=F32)


def tn(a, b):
    return lax.dot_general(a, b, (((0,), (0,)), ((), ())), preferred_element_type=F32)


def lanes(shape):
    return lax.broadcasted_iota(jnp.int32, shape, 1)


def swap_blocks(tiles):
    flat = tiles.reshape(128, 128)
    turned = [flat if s == 0 else pltpu.roll(flat, s * 16, 1) for s in range(8)]
    block = lanes((16, 128)) // 16
    out = []
    for j in range(8):
        tile = turned[(0 - j) % 8][0:16]
        for i in range(1, 8):
            tile = jnp.where(block == i, turned[(i - j) % 8][i * 16 : i * 16 + 16], tile)
        out.append(tile)
    return out


def in_layer(width, dy, dz):
    cell = lanes((16, width))
    row = (cell // 16) % 16 + dy
    col = cell % 16 + dz
    return (row >= 0) & (row < 16) & (col >= 0) & (col < 16)


def whole_kernel(
    f_in, ss_in, rs_in, cot_in, wb_in, w2_in, ow_in,
    bo_ref, gf_ref, vv_ref,
    f_ref, ss_ref, rs_ref, cot_ref, wb_ref, w2_ref, ow_ref,
    onehot, pick, fx, hx, hl, fm, fc, wt, aw, w9, s27, s9c, layer, s1acc,
    s1, a1, t1, a2, gw, cw, mine2, ww,
    kvt, qq, gg, qkv, gaw, lg, pr, sc, pk, acc, big, xs, ys, u1, alive, v1, d1,
    glw, gx, hf, hl2, hg, vs, e0, half, pair, quad, own64, zsrc, zall, back64, back256,
    in_sem, ex_s, ex_r, halo_s, halo_r, red_s, red_r,
):
    z = lax.axis_index("vox_0")
    x = lax.axis_index("vox_1")
    core = lax.axis_index("vox_2")
    xc = x * 2 + core
    y = lax.axis_index("ch")
    d = z * 8 + xc

    def to_y(p):
        return {"ch": p}

    def to_z(p):
        return {"vox_0": p}

    def to_x(p):
        return {"vox_1": p}

    def to_xc(p):
        return {"vox_1": p // 2, "vox_2": lax.rem(p, 2)}

    def to_d(p):
        return {"vox_0": p // 8, "vox_1": lax.rem(p, 8) // 2, "vox_2": lax.rem(p, 2)}

    after, before = lax.rem(d + 1, 64), lax.rem(d + 63, 64)

    loads = [
        pltpu.make_async_copy(src, dst, in_sem.at[i])
        for i, (src, dst) in enumerate(
            (
                (ss_in, ss_ref), (f_in, f_ref), (wb_in, wb_ref), (rs_in, rs_ref),
                (cot_in, cot_ref), (w2_in, w2_ref), (ow_in, ow_ref),
            )
        )
    ]
    for load in loads:
        load.start()

    barrier = pltpu.get_barrier_semaphore()
    for r in range(1, 8):
        for me, where in ((y, to_y), (z, to_z), (xc, to_xc)):
            pl.semaphore_signal(
                barrier, inc=1, device_id=where(lax.rem(me + r, 8)), device_id_type=MESH
            )
    for p in (after, before):
        pl.semaphore_signal(barrier, inc=1, device_id=to_d(p), device_id_type=MESH)

    fresh, old = [], []

    def send(src, dst, s_sem, r_sem, where):
        copy = pltpu.make_async_remote_copy(
            src_ref=src, dst_ref=dst, send_sem=s_sem, recv_sem=r_sem,
            device_id=where, device_id_type=MESH,
        )
        copy.start()
        fresh.append(copy)
        return copy

    def drain():
        for copy in old:
            copy.wait_send()
        old[:] = fresh
        fresh.clear()

    def exchange(phase, me, where, src_of, dst):
        copies = []
        for r in ORDER:
            p = lax.rem(me + r, 8)
            copies.append(
                send(src_of(p), dst, ex_s.at[phase, r], ex_r.at[phase, r], where(p))
            )
        return copies

    def arrive(copies):
        for copy in copies:
            copy.wait_recv()

    def rows16(b):
        return pl.ds(pl.multiple_of(b * 16, 16), 16)

    def tile(b):
        return pl.ds(pl.multiple_of(b * 128, 128), 128)

    def span(i, start=0, size=512):
        return pl.ds(pl.multiple_of(i * 512 + start, 256), size)

    mine = rows16(y)
    loads[0].wait()

    def onehot_step(i, carry):
        at = pl.multiple_of(i * 16, 16)
        ids = lax.broadcasted_iota(jnp.int32, (16, CELLS), 0) + at
        onehot[pl.ds(at, 16), :] = jnp.where(ids == ss_ref[...], 1.0, 0.0).astype(BF)
        return carry

    lax.fori_loop(0, 64, onehot_step, 0)

    loads[1].wait()
    fm[...] = jnp.where(ss_ref[...] >= 0, f_ref[...].astype(F32), 0.0).astype(BF)

    loads[2].wait()
    weights = jnp.concatenate([wb_ref[...].astype(F32), jnp.zeros((80, 128), F32)], axis=0)
    for t in range(4):
        wt[:, t * 128 : t * 128 + 128] = weights[t * 128 : t * 128 + 128, :].T.astype(BF)

    pl.semaphore_wait(barrier, 23)
    halo = [
        send(fm.at[:, CELLS - LAYER : CELLS], hl.at[0], halo_s.at[0], halo_r.at[0], to_d(after)),
        send(fm.at[:, 0:LAYER], hl.at[1], halo_s.at[1], halo_r.at[1], to_d(before)),
    ]
    got_aw = exchange(11, y, to_y, lambda p: wt.at[rows16(p), :], aw.at[y])
    def compact_step(i, carry):
        at = pl.multiple_of(i * 256, 256)
        fc[mine, pl.ds(at, 256)] = nt(fm[...], onehot[pl.ds(at, 256), :]).astype(BF)
        return carry


    lax.fori_loop(0, 2, compact_step, 0)
    got = exchange(0, y, to_y, lambda p: fc.at[mine, 0:512], fc.at[mine, 0:512])
    lax.fori_loop(2, 4, compact_step, 0)
    got += exchange(15, y, to_y, lambda p: fc.at[mine, 512:SLOTS], fc.at[mine, 512:SLOTS])

    aw[y] = wt[mine, :]
    for load in loads[3:]:
        load.wait()
    live = rs_ref[...] >= 0
    mine2[0:48, :] = w2_ref[...]
    mine2[48:64, :] = ow_ref[...]
    ww[y] = mine2[...]
    source = rs_ref[...]
    route = (source >> 4) & 7
    spot = jnp.where(live, route * 128 + ((source >> 7) & 7) * 16 + (source & 15), -1)

    arrive(halo)
    hx[mine, 0:LAYER] = jnp.where(d == 0, 0.0, hl[0].astype(F32)).astype(BF)
    hx[mine, LAYER : 2 * LAYER] = jnp.where(d == 63, 0.0, hl[1].astype(F32)).astype(BF)
    got_hx = exchange(12, y, to_y, lambda p: hx.at[mine, :], hx.at[mine, :])

    taps = [(dy, dz) for dy in (-1, 0, 1) for dz in (-1, 0, 1)]

    def shifted(values, width, put):
        for j, (dy, dz) in enumerate(taps):
            shift = -(dy * 16 + dz) % width
            slab = pltpu.roll(values, shift, 1) if shift else values
            slab = jnp.where(in_layer(width, dy, dz), slab, 0.0).astype(BF)
            for dx in range(3):
                put(dx, dx * 144 + j * 16, slab)

    def shifted_step(i, carry):
        def put(dx, row, slab):
            s27[row : row + 16, span(i, (3 - dx) * LAYER)] = slab

        shifted(fm[:, span(i)].astype(F32), 512, put)
        return carry

    lax.fori_loop(0, 8, shifted_step, 0)
    edges = hx[mine, :].astype(F32)

    def put_left(dx, row, slab):
        s27[row : row + 16, (2 - dx) * LAYER : (3 - dx) * LAYER] = slab[:, 0:LAYER]

    def put_right(dx, row, slab):
        s27[row : row + 16, (19 - dx) * LAYER : (20 - dx) * LAYER] = slab[:, LAYER : 2 * LAYER]

    shifted(edges, 512, put_left)
    shifted(edges, 512, put_right)

    def s9c_step(i, carry):
        at = pl.multiple_of(i * 256, 256)
        s9c[:, pl.ds(at, 256)] = nt(
            s27[:, 512 : 512 + CELLS], onehot[pl.ds(at, 256), :]
        ).astype(BF)
        return carry

    def pick_step(i, carry):
        at = pl.multiple_of(i * 16, 16)
        ids = lax.broadcasted_iota(jnp.int32, (16, SLOTS), 0) + at
        pick[pl.ds(at, 16), :] = jnp.where(ids == spot, 1.0, 0.0).astype(BF)
        return carry

    lax.fori_loop(0, 64, pick_step, 0)
    masked = jnp.where(live, cot_ref[...].astype(F32), 0.0).astype(BF)
    first = lax.broadcasted_iota(jnp.int32, (16, SLOTS), 0) == 0
    moved = jnp.concatenate([masked, jnp.where(first, 1.0, 0.0).astype(BF)], axis=0)
    moved = nt(moved, pick[...])
    cw[mine, :] = moved[0:16].astype(BF)
    alive[...] = moved[16:32]
    qq[...] = jnp.zeros((128, SLOTS), BF)
    gg[...] = jnp.zeros((128, SLOTS), BF)
    s1acc[...] = jnp.zeros((16, SLOTS), F32)
    acc[...] = jnp.zeros((32, SLOTS), F32)

    arrive(got_aw)
    for t in range(4):
        for k, part in enumerate(swap_blocks(aw[:, :, t * 128 : t * 128 + 128].astype(F32))):
            if t * 8 + k < 27:
                at = (t * 8 + k) * 16
                w9[at : at + 16, :] = part.astype(BF)

    arrive(got)
    got_ww = exchange(1, y, to_y, lambda p: mine2, ww.at[y])
    got_cw = exchange(2, y, to_y, lambda p: cw.at[mine, :], cw.at[mine, :])
    drain()

    def expand(src, dst, i):
        dst[:, span(i, LAYER)] = nn(src[...], onehot[:, span(i)]).astype(BF)

    def conv(i):
        total = None
        for dx in range(3):
            field = fx[:, span(i, dx * LAYER)]
            term = nn(w9[dx * 144 : dx * 144 + 144, :], field)
            total = term if total is None else total + term
        out = fm[:, span(i)].astype(F32)
        summed = jnp.zeros((16, 512), F32)
        for j, (dy, dz) in enumerate(taps):
            shift = -(dy * 16 + dz) % 512
            slab = total[j * 16 : j * 16 + 16]
            slab = pltpu.roll(slab, shift, 1) if shift else slab
            summed = summed + jnp.where(in_layer(512, dy, dz), slab, 0.0)
        layer[:, span(i)] = (out + summed).astype(BF)

    def pack(i):
        s1acc[...] += nt(layer[:, span(i)], onehot[:, span(i)])

    for i in range(4):
        expand(fc, fx, i)
    conv(1)

    def conv_step(i, carry):
        pack(i - 1)
        conv(i)
        expand(fc, fx, i + 2)
        return carry

    lax.fori_loop(2, 6, conv_step, 0)
    pack(5)
    conv(6)
    pack(6)
    arrive(got_hx)
    fx[:, 0:LAYER] = hx[:, 0:LAYER]
    fx[:, LAYER + CELLS : EXT] = hx[:, LAYER : 2 * LAYER]
    conv(0)
    pack(0)
    conv(7)
    pack(7)
    packed = s1acc[...].astype(BF)
    for t in range(8):
        s1[t] = packed[:, t * 128 : t * 128 + 128]
    a1[z] = s1[z]
    got = exchange(3, z, to_z, lambda p: s1.at[p], a1.at[z])
    lax.fori_loop(0, 2, s9c_step, 0)

    drain()
    arrive(got)
    for j, part in enumerate(swap_blocks(a1[...].astype(F32))):
        t1[j] = part.astype(BF)
    a2[xc] = t1[xc]
    got = exchange(4, xc, to_xc, lambda p: t1.at[p], a2.at[xc])
    drain()
    arrive(got)
    arrived = jnp.concatenate([a2[i] for i in range(8)], axis=1)
    gw[mine, :] = arrived
    got = exchange(5, y, to_y, lambda p: gw.at[mine, :], gw.at[mine, :])
    drain()
    arrive(got_cw)
    arrive(got_ww)
    ga = nn(ow_ref[...], cw[...]).astype(BF)
    gaw[...] = ga
    gg[32:48, :] = (ga.astype(F32) * 0.25).astype(BF)
    lax.fori_loop(2, 4, s9c_step, 0)
    arrive(got)

    whole = gw[...].astype(F32)
    mean = jnp.mean(whole, axis=0, keepdims=True)
    centred = whole - mean
    var = jnp.mean(centred * centred, axis=0, keepdims=True)
    normed = (centred * lax.rsqrt(var + 1e-05)).astype(BF)
    big[...] = normed
    rows = nn(w2_ref[...], normed).astype(BF)
    qkv[...] = rows
    qq[0:16, :] = (rows[0:16].astype(F32) * 0.25).astype(BF)
    row = lax.broadcasted_iota(jnp.int32, (16, SLOTS), 0)
    qq[16:32, :] = jnp.where(row == 0, 1.0, 0.0).astype(BF)
    bias = jnp.where((row == 0) & (alive[...] < 0.5), -1e30, 0.0)
    stacked = jnp.concatenate(
        [
            rows[16:32].astype(F32),
            bias,
            rows[32:48].astype(F32),
            jnp.zeros((80, SLOTS), F32),
        ],
        axis=0,
    )
    for t in range(8):
        kvt[t * 128 : t * 128 + 128, :] = stacked[:, t * 128 : t * 128 + 128].T.astype(BF)

    def attend_step(i, carry):
        at = pl.ds(pl.multiple_of(i * 256, 256), 256)
        top = None
        for c in range(4):
            cells = slice(c * 256, c * 256 + 256)
            logits = nn(kvt[cells, :], qq[:, at])
            lg[cells, :] = logits
            most = jnp.max(logits.reshape(32, 8, 256), axis=0)
            top = most if top is None else jnp.maximum(top, most)
        top = jnp.max(top, axis=0, keepdims=True)
        total = jnp.zeros((8, 256), F32)
        for c in range(16):
            cells = slice(c * 64, c * 64 + 64)
            exponents = jnp.exp(lg[cells, :] - top)
            lg[cells, :] = exponents
            total = total + jnp.sum(exponents.reshape(8, 8, 256), axis=0)
        inverse_total = 1.0 / jnp.sum(total, axis=0, keepdims=True)
        for c in range(16):
            cells = slice(c * 64, c * 64 + 64)
            pr[cells, :] = (lg[cells, :] * inverse_total).astype(BF)
        attended = nn(qkv[32:48, :], pr[...])
        pk[0:16, at] = attended.astype(BF)
        inner = jnp.sum(attended * gg[32:48, at].astype(F32), axis=0, keepdims=True)
        acc[16:32, :] += nt(gaw[:, at], pr[...])
        for c in range(4):
            cells = slice(c * 256, c * 256 + 256)
            grad_logits = nn(kvt[cells, :], gg[:, at])
            sc[cells, :] = (pr[cells, :].astype(F32) * (grad_logits - inner)).astype(BF)
        pk[16:32, at] = nn(qkv[16:32, :], sc[...]).astype(BF)
        acc[0:16, :] += nt(qkv[0:16, at], sc[...])
        return carry

    lax.fori_loop(0, 4, attend_step, 0)
    pk[32:64, :] = acc[...].astype(BF)

    ys[y] = pk[:, tile(y)]
    got = exchange(6, y, to_y, lambda p: pk.at[:, tile(p)], ys.at[y])
    drain()
    vs[432:480, :] = nt(pk[16:64, :], big[...])
    vs[480:496, :] = nt(pk[0:16, :], cw[...])
    vs[496:512, :] = jnp.zeros((16, 128), F32)
    own_slots = tile(y)
    part = gw[:, own_slots].astype(F32)
    mean = jnp.mean(part, axis=0, keepdims=True)
    centred = part - mean
    var = jnp.mean(centred * centred, axis=0, keepdims=True)
    inverse = lax.rsqrt(var + 1e-05)
    normal = centred * inverse
    cot = cw[:, own_slots].astype(F32)
    live_part = alive[0:1, own_slots] > 0.5
    arrive(got)
    mixed = tn(ww[:, 48:64, :].reshape(128, 128), ys[:, 0:16, :].reshape(128, 128))
    grad = None
    for i in range(3):
        term = tn(
            ww[:, i * 16 : i * 16 + 16, :].reshape(128, 128),
            ys[:, 16 + i * 16 : 32 + i * 16, :].reshape(128, 128),
        )
        grad = term if grad is None else grad + term
    grad = grad.astype(BF).astype(F32)
    grad_ln = inverse * (
        grad
        - jnp.mean(grad, axis=0, keepdims=True)
        - normal * jnp.mean(grad * normal, axis=0, keepdims=True)
    )
    back = jnp.where(live_part, cot + grad_ln, 0.0).astype(BF)
    block = jnp.where(live_part, part + mixed, 0.0).astype(BF)
    xs[:, 0:16, :] = back.reshape(8, 16, 128)
    xs[:, 16:32, :] = block.reshape(8, 16, 128)
    u1[y] = xs[y]
    got = exchange(7, y, to_y, lambda p: xs.at[p], u1.at[y])
    drain()
    arrive(got)
    v1[xc] = u1[xc, 0:16, :]
    got = exchange(8, xc, to_xc, lambda p: u1.at[p, 0:16, :], v1.at[xc])
    drain()
    bo_ref[...] = nn(jnp.concatenate([u1[i, 16:32] for i in range(8)], axis=1), pick[...]).astype(BF)
    arrive(got)
    for j, piece in enumerate(swap_blocks(v1[...].astype(F32))):
        d1[j] = piece.astype(BF)
    e0[z] = d1[z]
    got = exchange(9, z, to_z, lambda p: d1.at[p], e0.at[z])
    drain()
    arrive(got)
    slots = jnp.concatenate([e0[i] for i in range(8)], axis=1)
    glw[mine, :] = slots
    got = exchange(10, y, to_y, lambda p: glw.at[mine, :], glw.at[mine, :])
    drain()
    hf[:, 0:LAYER] = nn(slots, onehot[:, 0:LAYER]).astype(BF)
    hf[:, LAYER : 2 * LAYER] = nn(slots, onehot[:, CELLS - LAYER : CELLS]).astype(BF)
    halo = [
        send(hf.at[:, LAYER : 2 * LAYER], hl2.at[0], halo_s.at[2], halo_r.at[2], to_d(after)),
        send(hf.at[:, 0:LAYER], hl2.at[1], halo_s.at[3], halo_r.at[3], to_d(before)),
    ]
    arrive(halo)
    hg[mine, 0:LAYER] = jnp.where(d == 0, 0.0, hl2[0].astype(F32)).astype(BF)
    hg[mine, LAYER : 2 * LAYER] = jnp.where(d == 63, 0.0, hl2[1].astype(F32)).astype(BF)
    got_halo = exchange(13, y, to_y, lambda p: hg.at[mine, :], hg.at[mine, :])
    arrive(got)

    vs[0:432, :] = nt(s9c[...], glw[...])

    def rows64(b):
        return pl.ds(pl.multiple_of(b * 64, 64), 64)

    def rows256(b):
        return pl.ds(pl.multiple_of(b * 256, 256), 256)

    def grad_expand(i, carry):
        expand(glw, gx, i)
        return carry

    def input_step(i, carry):
        total = None
        for dx in range(3):
            field = gx[:, span(i, (2 - dx) * LAYER)]
            term = nn(wb_ref[dx * 144 : dx * 144 + 144, :], field)
            total = term if total is None else total + term
        conv = jnp.zeros((16, 512), F32)
        for j, (dy, dz) in enumerate(taps):
            shift = (dy * 16 + dz) % 512
            slab = total[j * 16 : j * 16 + 16]
            slab = pltpu.roll(slab, shift, 1) if shift else slab
            conv = conv + jnp.where(in_layer(512, -dy, -dz), slab, 0.0)
        own_grad = gx[mine, span(i, LAYER)].astype(F32)
        gf_ref[:, span(i)] = own_grad + jnp.where(ss_ref[:, span(i)] >= 0, conv, 0.0)
        return carry

    def pair_send(src, dst, n):
        return send(src, dst, red_s.at[n], red_r.at[n], {"vox_2": 1 - core})

    def x_send(src_of, dst, n):
        copies = []
        for r in (2, 1, 3):
            p = lax.rem(x + r, 4)
            copies.append(send(src_of(p), dst, red_s.at[n + r], red_r.at[n + r], to_x(p)))
        return copies

    got = [pair_send(vs.at[rows256(1 - core), :], half, 0)]
    arrive(got)
    pair[...] = vs[rows256(core), :] + half[...]
    quad[x] = pair[rows64(x), :]
    got = x_send(lambda p: pair.at[rows64(p), :], quad.at[x], 0)
    drain()
    lax.fori_loop(0, 8, grad_expand, 0)
    arrive(got)
    own64[...] = (quad[0] + quad[1] + quad[2] + quad[3]).astype(BF)
    zsrc[z] = own64[...]
    got = exchange(14, z, to_z, lambda p: own64, zsrc.at[z])
    drain()
    arrive(got_halo)
    gx[:, 0:LAYER] = hg[:, 0:LAYER]
    gx[:, LAYER + CELLS : EXT] = hg[:, LAYER : 2 * LAYER]
    lax.fori_loop(0, 6, input_step, 0)
    arrive(got)
    total = zsrc[0].astype(F32)
    for i in range(1, 8):
        total = total + zsrc[i].astype(F32)
    zall[...] = total
    back256[rows64(x), :] = total
    got = x_send(lambda p: zall, back256.at[rows64(x), :], 4)
    lax.fori_loop(6, 8, input_step, 0)
    drain()
    arrive(got)
    got = [pair_send(back256, back64, 8)]
    vv_ref[rows256(core), :] = back256[...]
    drain()
    arrive(got)
    vv_ref[rows256(1 - core), :] = back64[...]
    drain()
    drain()


def store_kernel(bo_ref, gf_ref, vv_ref, bo_out, gf_out, gc_out, gq_out, go_out, sem):
    stores = [
        pltpu.make_async_copy(src, dst, sem.at[i])
        for i, (src, dst) in enumerate(
            (
                (gf_ref, gf_out), (vv_ref.at[0:432, :], gc_out), (vv_ref.at[432:480, :], gq_out),
                (vv_ref.at[480:496, :], go_out), (bo_ref, bo_out),
            )
        )
    ]
    for store in stores:
        store.start()
    for store in stores:
        store.wait()


def body(
    features, conv_weight, qkv_weight, out_weight, cotangent, neighbours, send_slot, recv_slot
):
    wb = jnp.transpose(conv_weight, (0, 2, 1)).reshape(432, 128)
    w2 = jnp.transpose(qkv_weight, (0, 2, 1)).reshape(48, 128)

    def buf(*shape):
        return pltpu.VMEM(shape, BF)

    def wide(*shape):
        return pltpu.VMEM(shape, F32)

    scratch = [
        buf(16, CELLS), pltpu.VMEM((1, CELLS), jnp.int32), pltpu.VMEM((1, SLOTS), jnp.int32),
        buf(16, SLOTS), buf(432, 128), buf(48, 128), buf(16, 128),
        buf(SLOTS, CELLS), buf(SLOTS, SLOTS),
        buf(128, EXT), buf(128, 512), buf(2, 16, LAYER), buf(16, CELLS),
        buf(128, SLOTS), buf(128, 512), buf(8, 16, 512), buf(432, 128),
        buf(432, 20 * LAYER), buf(432, SLOTS), buf(16, CELLS), wide(16, SLOTS),
        buf(8, 16, 128), buf(8, 16, 128), buf(8, 16, 128), buf(8, 16, 128),
        buf(128, SLOTS), buf(128, SLOTS), buf(64, 128), buf(8, 64, 128),
        buf(SLOTS, 128), buf(128, SLOTS), buf(128, SLOTS), buf(48, SLOTS),
        buf(16, SLOTS), wide(SLOTS, 256), buf(SLOTS, 256), buf(SLOTS, 256),
        buf(64, SLOTS), wide(32, SLOTS), buf(128, SLOTS),
        buf(8, 32, 128), buf(8, 64, 128), buf(8, 32, 128),
        wide(16, SLOTS), buf(8, 16, 128), buf(8, 16, 128),
        buf(128, SLOTS), buf(128, EXT), buf(16, 512), buf(2, 16, LAYER), buf(128, 512),
        wide(512, 128), buf(8, 16, 128), wide(256, 128), wide(256, 128),
        wide(4, 64, 128), buf(64, 128), buf(8, 64, 128), wide(64, 128),
        wide(256, 128), wide(256, 128),
        pltpu.SemaphoreType.DMA((7,)),
        pltpu.SemaphoreType.DMA((16, 8)), pltpu.SemaphoreType.DMA((16, 8)),
        pltpu.SemaphoreType.DMA((4,)), pltpu.SemaphoreType.DMA((4,)),
        pltpu.SemaphoreType.DMA((9,)), pltpu.SemaphoreType.DMA((9,)),
    ]
    hbm = pl.BlockSpec(memory_space=pltpu.HBM)
    vmem = pl.BlockSpec(memory_space=pltpu.VMEM)
    block_out, grad_features, sums = pl.pallas_call(
        whole_kernel,
        out_shape=(
            jax.ShapeDtypeStruct((16, SLOTS), BF),
            jax.ShapeDtypeStruct((16, CELLS), F32),
            jax.ShapeDtypeStruct((512, 128), F32),
        ),
        in_specs=[hbm] * 7,
        out_specs=(vmem, vmem, vmem),
        scratch_shapes=scratch,
        compiler_params=pltpu.CompilerParams(
            collective_id=0, has_side_effects=True, vmem_limit_bytes=48 * 1024 * 1024
        ),
    )(
        *(
            pltpu.with_memory_space_constraint(array, pltpu.HBM)
            for array in (
                features, send_slot.reshape(1, CELLS), recv_slot.reshape(1, SLOTS), cotangent,
                wb, w2, out_weight,
            )
        )
    )
    block_out, grad_features, grad_conv, grad_qkv, grad_out = pl.pallas_call(
        store_kernel,
        out_shape=(
            jax.ShapeDtypeStruct((16, SLOTS), BF),
            jax.ShapeDtypeStruct((16, CELLS), F32),
            jax.ShapeDtypeStruct((432, 128), F32),
            jax.ShapeDtypeStruct((48, 128), F32),
            jax.ShapeDtypeStruct((16, 128), F32),
        ),
        in_specs=[vmem] * 3,
        out_specs=(hbm,) * 5,
        scratch_shapes=[pltpu.SemaphoreType.DMA((5,))],
        compiler_params=pltpu.CompilerParams(vmem_limit_bytes=4 * 1024 * 1024),
    )(block_out, grad_features, sums)
    grad_conv = jnp.transpose(grad_conv.reshape(27, 16, 128), (0, 2, 1))
    grad_qkv = jnp.transpose(grad_qkv.reshape(3, 16, 128), (0, 2, 1))
    return (block_out, grad_features, grad_conv, grad_qkv, grad_out)


def solution(mesh):
    torus = Mesh(mesh.devices.reshape(8, 4, 2, mesh.shape["ch"]), ("vox_0", "vox_1", "vox_2", "ch"))
    placed = (
        P("ch", VOX),
        P(None, None, "ch"),
        P(None, None, "ch"),
        P("ch", None),
        P("ch", VOX),
        P(None, VOX),
        P(VOX),
        P(VOX),
    )
    return jax.shard_map(
        body,
        mesh=torus,
        in_specs=placed,
        out_specs=(
            P("ch", VOX),
            P("ch", VOX),
            P(None, None, "ch"),
            P(None, None, "ch"),
            P("ch", None),
        ),
        check_vma=False,
    )
```

```python
import jax
import jax.numpy as jnp
from jax import lax
from jax.experimental import pallas as pl
from jax.experimental.pallas import tpu as pltpu
from jax.sharding import Mesh
from jax.sharding import PartitionSpec as P

MESH = pl.DeviceIdType.MESH
VOX = ("vox_0", "vox_1", "vox_2")
BF = jnp.bfloat16
F32 = jnp.float32
CELLS = 4096
LAYER = 256
EXT = CELLS + 2 * LAYER
SLOTS = 1024
ORDER = (4, 3, 5, 2, 6, 1, 7)


def nn(a, b):
    return jnp.dot(a, b, preferred_element_type=F32)


def nt(a, b):
    return lax.dot_general(a, b, (((1,), (1,)), ((), ())), preferred_element_type=F32)


def tn(a, b):
    return lax.dot_general(a, b, (((0,), (0,)), ((), ())), preferred_element_type=F32)


def lanes(shape):
    return lax.broadcasted_iota(jnp.int32, shape, 1)


def swap_blocks(tiles):
    flat = tiles.reshape(128, 128)
    turned = [flat if s == 0 else pltpu.roll(flat, s * 16, 1) for s in range(8)]
    block = lanes((16, 128)) // 16
    out = []
    for j in range(8):
        tile = turned[(0 - j) % 8][0:16]
        for i in range(1, 8):
            tile = jnp.where(block == i, turned[(i - j) % 8][i * 16 : i * 16 + 16], tile)
        out.append(tile)
    return out


def in_layer(width, dy, dz):
    cell = lanes((16, width))
    row = (cell // 16) % 16 + dy
    col = cell % 16 + dz
    return (row >= 0) & (row < 16) & (col >= 0) & (col < 16)


def whole_kernel(
    f_in, ss_in, rs_in, cot_in, wb_in, w2_in, ow_in,
    bo_ref, gf_ref, vv_ref,
    f_ref, ss_ref, rs_ref, cot_ref, wb_ref, w2_ref, ow_ref,
    onehot, pick, fx, hx, hl, fm, fc, wt, aw, w9, s27, s9c, layer, s1acc,
    s1, a1, t1, a2, gw, cw, mine2, ww,
    kvt, qq, gg, qkv, gaw, lg, pr, sc, pk, acc, big, xs, ys, u1, alive, v1, d1,
    glw, gx, hf, hl2, hg, vs, e0, half, pair, quad, own64, zsrc, zall, back64, back256,
    pattern, high,
    in_sem, ex_s, ex_r, halo_s, halo_r, red_s, red_r,
):
    z = lax.axis_index("vox_0")
    x = lax.axis_index("vox_1")
    core = lax.axis_index("vox_2")
    xc = x * 2 + core
    y = lax.axis_index("ch")
    d = z * 8 + xc

    def to_y(p):
        return {"ch": p}

    def to_z(p):
        return {"vox_0": p}

    def to_x(p):
        return {"vox_1": p}

    def to_xc(p):
        return {"vox_1": p // 2, "vox_2": lax.rem(p, 2)}

    def to_d(p):
        return {"vox_0": p // 8, "vox_1": lax.rem(p, 8) // 2, "vox_2": lax.rem(p, 2)}

    after, before = lax.rem(d + 1, 64), lax.rem(d + 63, 64)

    loads = [
        pltpu.make_async_copy(src, dst, in_sem.at[i])
        for i, (src, dst) in enumerate(
            (
                (ss_in, ss_ref), (f_in, f_ref), (wb_in, wb_ref), (rs_in, rs_ref),
                (cot_in, cot_ref), (w2_in, w2_ref), (ow_in, ow_ref),
            )
        )
    ]
    for load in loads:
        load.start()

    barrier = pltpu.get_barrier_semaphore()
    for r in range(1, 8):
        for me, where in ((y, to_y), (z, to_z), (xc, to_xc)):
            pl.semaphore_signal(
                barrier, inc=1, device_id=where(lax.rem(me + r, 8)), device_id_type=MESH
            )
    for p in (after, before):
        pl.semaphore_signal(barrier, inc=1, device_id=to_d(p), device_id_type=MESH)

    fresh, old = [], []

    def send(src, dst, s_sem, r_sem, where):
        copy = pltpu.make_async_remote_copy(
            src_ref=src, dst_ref=dst, send_sem=s_sem, recv_sem=r_sem,
            device_id=where, device_id_type=MESH,
        )
        copy.start()
        fresh.append(copy)
        return copy

    def drain():
        for copy in old:
            copy.wait_send()
        old[:] = fresh
        fresh.clear()

    def exchange(phase, me, where, src_of, dst):
        copies = []
        for r in ORDER:
            p = lax.rem(me + r, 8)
            copies.append(
                send(src_of(p), dst, ex_s.at[phase, r], ex_r.at[phase, r], where(p))
            )
        return copies

    def arrive(copies):
        for copy in copies:
            copy.wait_recv()

    def rows16(b):
        return pl.ds(pl.multiple_of(b * 16, 16), 16)

    def tile(b):
        return pl.ds(pl.multiple_of(b * 128, 128), 128)

    def span(i, start=0, size=512):
        return pl.ds(pl.multiple_of(i * 512 + start, 256), size)

    mine = rows16(y)
    loads[0].wait()

    low = lax.broadcasted_iota(jnp.int32, (16, CELLS), 0)
    pattern[...] = jnp.where(low == (ss_ref[...] & 15), 1.0, 0.0).astype(BF)
    high[...] = jnp.broadcast_to((ss_ref[...] >> 4).astype(F32), (16, CELLS)).astype(BF)

    def onehot_step(i, carry):
        at = pl.multiple_of(i * 16, 16)
        here = high[...] == i.astype(F32).astype(BF)
        onehot[pl.ds(at, 16), :] = jnp.where(here, pattern[...], jnp.zeros((), BF))
        return carry

    lax.fori_loop(0, 64, onehot_step, 0)

    loads[1].wait()
    fm[...] = jnp.where(ss_ref[...] >= 0, f_ref[...].astype(F32), 0.0).astype(BF)

    loads[2].wait()
    weights = jnp.concatenate([wb_ref[...].astype(F32), jnp.zeros((80, 128), F32)], axis=0)
    for t in range(4):
        wt[:, t * 128 : t * 128 + 128] = weights[t * 128 : t * 128 + 128, :].T.astype(BF)

    pl.semaphore_wait(barrier, 23)
    halo = [
        send(fm.at[:, CELLS - LAYER : CELLS], hl.at[0], halo_s.at[0], halo_r.at[0], to_d(after)),
        send(fm.at[:, 0:LAYER], hl.at[1], halo_s.at[1], halo_r.at[1], to_d(before)),
    ]
    got_aw = exchange(11, y, to_y, lambda p: wt.at[rows16(p), :], aw.at[y])
    def compact_step(i, carry):
        at = pl.multiple_of(i * 256, 256)
        fc[mine, pl.ds(at, 256)] = nt(fm[...], onehot[pl.ds(at, 256), :]).astype(BF)
        return carry


    lax.fori_loop(0, 2, compact_step, 0)
    got = exchange(0, y, to_y, lambda p: fc.at[mine, 0:512], fc.at[mine, 0:512])
    lax.fori_loop(2, 4, compact_step, 0)
    got += exchange(15, y, to_y, lambda p: fc.at[mine, 512:SLOTS], fc.at[mine, 512:SLOTS])

    aw[y] = wt[mine, :]
    for load in loads[3:]:
        load.wait()
    live = rs_ref[...] >= 0
    mine2[0:48, :] = w2_ref[...]
    mine2[48:64, :] = ow_ref[...]
    ww[y] = mine2[...]
    source = rs_ref[...]
    route = (source >> 4) & 7
    spot = jnp.where(live, route * 128 + ((source >> 7) & 7) * 16 + (source & 15), -1)

    arrive(halo)
    hx[mine, 0:LAYER] = jnp.where(d == 0, 0.0, hl[0].astype(F32)).astype(BF)
    hx[mine, LAYER : 2 * LAYER] = jnp.where(d == 63, 0.0, hl[1].astype(F32)).astype(BF)
    got_hx = exchange(12, y, to_y, lambda p: hx.at[mine, :], hx.at[mine, :])

    taps = [(dy, dz) for dy in (-1, 0, 1) for dz in (-1, 0, 1)]

    def shifted(values, width, put):
        for j, (dy, dz) in enumerate(taps):
            shift = -(dy * 16 + dz) % width
            slab = pltpu.roll(values, shift, 1) if shift else values
            slab = jnp.where(in_layer(width, dy, dz), slab, 0.0).astype(BF)
            for dx in range(3):
                put(dx, dx * 144 + j * 16, slab)

    def shifted_step(i, carry):
        def put(dx, row, slab):
            s27[row : row + 16, span(i, (3 - dx) * LAYER)] = slab

        shifted(fm[:, span(i)].astype(F32), 512, put)
        return carry

    lax.fori_loop(0, 8, shifted_step, 0)
    edges = hx[mine, :].astype(F32)

    def put_left(dx, row, slab):
        s27[row : row + 16, (2 - dx) * LAYER : (3 - dx) * LAYER] = slab[:, 0:LAYER]

    def put_right(dx, row, slab):
        s27[row : row + 16, (19 - dx) * LAYER : (20 - dx) * LAYER] = slab[:, LAYER : 2 * LAYER]

    shifted(edges, 512, put_left)
    shifted(edges, 512, put_right)

    def s9c_step(i, carry):
        at = pl.multiple_of(i * 256, 256)
        s9c[:, pl.ds(at, 256)] = nt(
            s27[:, 512 : 512 + CELLS], onehot[pl.ds(at, 256), :]
        ).astype(BF)
        return carry

    def pick_step(i, carry):
        at = pl.multiple_of(i * 16, 16)
        ids = lax.broadcasted_iota(jnp.int32, (16, SLOTS), 0) + at
        pick[pl.ds(at, 16), :] = jnp.where(ids == spot, 1.0, 0.0).astype(BF)
        return carry

    lax.fori_loop(0, 64, pick_step, 0)
    masked = jnp.where(live, cot_ref[...].astype(F32), 0.0).astype(BF)
    first = lax.broadcasted_iota(jnp.int32, (16, SLOTS), 0) == 0
    moved = jnp.concatenate([masked, jnp.where(first, 1.0, 0.0).astype(BF)], axis=0)
    moved = nt(moved, pick[...])
    cw[mine, :] = moved[0:16].astype(BF)
    alive[...] = moved[16:32]
    qq[...] = jnp.zeros((128, SLOTS), BF)
    gg[...] = jnp.zeros((128, SLOTS), BF)
    s1acc[...] = jnp.zeros((16, SLOTS), F32)
    acc[...] = jnp.zeros((32, SLOTS), F32)

    arrive(got_aw)
    for t in range(4):
        for k, part in enumerate(swap_blocks(aw[:, :, t * 128 : t * 128 + 128].astype(F32))):
            if t * 8 + k < 27:
                at = (t * 8 + k) * 16
                w9[at : at + 16, :] = part.astype(BF)

    arrive(got)
    got_ww = exchange(1, y, to_y, lambda p: mine2, ww.at[y])
    got_cw = exchange(2, y, to_y, lambda p: cw.at[mine, :], cw.at[mine, :])
    drain()

    def expand(src, dst, i):
        dst[:, span(i, LAYER)] = nn(src[...], onehot[:, span(i)]).astype(BF)

    def conv(i):
        total = None
        for dx in range(3):
            field = fx[:, span(i, dx * LAYER)]
            term = nn(w9[dx * 144 : dx * 144 + 144, :], field)
            total = term if total is None else total + term
        out = fm[:, span(i)].astype(F32)
        summed = jnp.zeros((16, 512), F32)
        for j, (dy, dz) in enumerate(taps):
            shift = -(dy * 16 + dz) % 512
            slab = total[j * 16 : j * 16 + 16]
            slab = pltpu.roll(slab, shift, 1) if shift else slab
            summed = summed + jnp.where(in_layer(512, dy, dz), slab, 0.0)
        layer[:, span(i)] = (out + summed).astype(BF)

    def pack(i):
        s1acc[...] += nt(layer[:, span(i)], onehot[:, span(i)])

    for i in range(4):
        expand(fc, fx, i)
    conv(1)

    def conv_step(i, carry):
        pack(i - 1)
        conv(i)
        expand(fc, fx, i + 2)
        return carry

    lax.fori_loop(2, 6, conv_step, 0)
    pack(5)
    conv(6)
    pack(6)
    arrive(got_hx)
    fx[:, 0:LAYER] = hx[:, 0:LAYER]
    fx[:, LAYER + CELLS : EXT] = hx[:, LAYER : 2 * LAYER]
    conv(0)
    pack(0)
    conv(7)
    pack(7)
    packed = s1acc[...].astype(BF)
    for t in range(8):
        s1[t] = packed[:, t * 128 : t * 128 + 128]
    a1[z] = s1[z]
    got = exchange(3, z, to_z, lambda p: s1.at[p], a1.at[z])
    lax.fori_loop(0, 2, s9c_step, 0)

    drain()
    arrive(got)
    for j, part in enumerate(swap_blocks(a1[...].astype(F32))):
        t1[j] = part.astype(BF)
    a2[xc] = t1[xc]
    got = exchange(4, xc, to_xc, lambda p: t1.at[p], a2.at[xc])
    drain()
    arrive(got)
    arrived = jnp.concatenate([a2[i] for i in range(8)], axis=1)
    gw[mine, :] = arrived
    got = exchange(5, y, to_y, lambda p: gw.at[mine, :], gw.at[mine, :])
    drain()
    arrive(got_cw)
    arrive(got_ww)
    ga = nn(ow_ref[...], cw[...]).astype(BF)
    gaw[...] = ga
    gg[32:48, :] = (ga.astype(F32) * 0.25).astype(BF)
    lax.fori_loop(2, 4, s9c_step, 0)
    arrive(got)

    whole = gw[...].astype(F32)
    mean = jnp.mean(whole, axis=0, keepdims=True)
    centred = whole - mean
    var = jnp.mean(centred * centred, axis=0, keepdims=True)
    normed = (centred * lax.rsqrt(var + 1e-05)).astype(BF)
    big[...] = normed
    rows = nn(w2_ref[...], normed).astype(BF)
    qkv[...] = rows
    qq[0:16, :] = (rows[0:16].astype(F32) * 0.25).astype(BF)
    row = lax.broadcasted_iota(jnp.int32, (16, SLOTS), 0)
    qq[16:32, :] = jnp.where(row == 0, 1.0, 0.0).astype(BF)
    bias = jnp.where((row == 0) & (alive[...] < 0.5), -1e30, 0.0)
    stacked = jnp.concatenate(
        [
            rows[16:32].astype(F32),
            bias,
            rows[32:48].astype(F32),
            jnp.zeros((80, SLOTS), F32),
        ],
        axis=0,
    )
    for t in range(8):
        kvt[t * 128 : t * 128 + 128, :] = stacked[:, t * 128 : t * 128 + 128].T.astype(BF)

    def attend_step(i, carry):
        at = pl.ds(pl.multiple_of(i * 256, 256), 256)
        top = None
        for c in range(4):
            cells = slice(c * 256, c * 256 + 256)
            logits = nn(kvt[cells, :], qq[:, at])
            lg[cells, :] = logits
            most = jnp.max(logits.reshape(32, 8, 256), axis=0)
            top = most if top is None else jnp.maximum(top, most)
        top = jnp.max(top, axis=0, keepdims=True)
        total = jnp.zeros((8, 256), F32)
        for c in range(16):
            cells = slice(c * 64, c * 64 + 64)
            exponents = jnp.exp(lg[cells, :] - top)
            lg[cells, :] = exponents
            total = total + jnp.sum(exponents.reshape(8, 8, 256), axis=0)
        inverse_total = 1.0 / jnp.sum(total, axis=0, keepdims=True)
        for c in range(16):
            cells = slice(c * 64, c * 64 + 64)
            pr[cells, :] = (lg[cells, :] * inverse_total).astype(BF)
        attended = nn(qkv[32:48, :], pr[...])
        pk[0:16, at] = attended.astype(BF)
        inner = jnp.sum(attended * gg[32:48, at].astype(F32), axis=0, keepdims=True)
        acc[16:32, :] += nt(gaw[:, at], pr[...])
        for c in range(4):
            cells = slice(c * 256, c * 256 + 256)
            grad_logits = nn(kvt[cells, :], gg[:, at])
            sc[cells, :] = (pr[cells, :].astype(F32) * (grad_logits - inner)).astype(BF)
        pk[16:32, at] = nn(qkv[16:32, :], sc[...]).astype(BF)
        acc[0:16, :] += nt(qkv[0:16, at], sc[...])
        return carry

    lax.fori_loop(0, 4, attend_step, 0)
    pk[32:64, :] = acc[...].astype(BF)

    ys[y] = pk[:, tile(y)]
    got = exchange(6, y, to_y, lambda p: pk.at[:, tile(p)], ys.at[y])
    drain()
    vs[432:480, :] = nt(pk[16:64, :], big[...])
    vs[480:496, :] = nt(pk[0:16, :], cw[...])
    vs[496:512, :] = jnp.zeros((16, 128), F32)
    own_slots = tile(y)
    part = gw[:, own_slots].astype(F32)
    mean = jnp.mean(part, axis=0, keepdims=True)
    centred = part - mean
    var = jnp.mean(centred * centred, axis=0, keepdims=True)
    inverse = lax.rsqrt(var + 1e-05)
    normal = centred * inverse
    cot = cw[:, own_slots].astype(F32)
    live_part = alive[0:1, own_slots] > 0.5
    arrive(got)
    mixed = tn(ww[:, 48:64, :].reshape(128, 128), ys[:, 0:16, :].reshape(128, 128))
    grad = None
    for i in range(3):
        term = tn(
            ww[:, i * 16 : i * 16 + 16, :].reshape(128, 128),
            ys[:, 16 + i * 16 : 32 + i * 16, :].reshape(128, 128),
        )
        grad = term if grad is None else grad + term
    grad = grad.astype(BF).astype(F32)
    grad_ln = inverse * (
        grad
        - jnp.mean(grad, axis=0, keepdims=True)
        - normal * jnp.mean(grad * normal, axis=0, keepdims=True)
    )
    back = jnp.where(live_part, cot + grad_ln, 0.0).astype(BF)
    block = jnp.where(live_part, part + mixed, 0.0).astype(BF)
    xs[:, 0:16, :] = back.reshape(8, 16, 128)
    xs[:, 16:32, :] = block.reshape(8, 16, 128)
    u1[y] = xs[y]
    got = exchange(7, y, to_y, lambda p: xs.at[p], u1.at[y])
    drain()
    arrive(got)
    v1[xc] = u1[xc, 0:16, :]
    got = exchange(8, xc, to_xc, lambda p: u1.at[p, 0:16, :], v1.at[xc])
    drain()
    bo_ref[...] = nn(jnp.concatenate([u1[i, 16:32] for i in range(8)], axis=1), pick[...]).astype(BF)
    arrive(got)
    for j, piece in enumerate(swap_blocks(v1[...].astype(F32))):
        d1[j] = piece.astype(BF)
    e0[z] = d1[z]
    got = exchange(9, z, to_z, lambda p: d1.at[p], e0.at[z])
    drain()
    arrive(got)
    slots = jnp.concatenate([e0[i] for i in range(8)], axis=1)
    glw[mine, :] = slots
    got = exchange(10, y, to_y, lambda p: glw.at[mine, :], glw.at[mine, :])
    drain()
    hf[:, 0:LAYER] = nn(slots, onehot[:, 0:LAYER]).astype(BF)
    hf[:, LAYER : 2 * LAYER] = nn(slots, onehot[:, CELLS - LAYER : CELLS]).astype(BF)
    halo = [
        send(hf.at[:, LAYER : 2 * LAYER], hl2.at[0], halo_s.at[2], halo_r.at[2], to_d(after)),
        send(hf.at[:, 0:LAYER], hl2.at[1], halo_s.at[3], halo_r.at[3], to_d(before)),
    ]
    arrive(halo)
    hg[mine, 0:LAYER] = jnp.where(d == 0, 0.0, hl2[0].astype(F32)).astype(BF)
    hg[mine, LAYER : 2 * LAYER] = jnp.where(d == 63, 0.0, hl2[1].astype(F32)).astype(BF)
    got_halo = exchange(13, y, to_y, lambda p: hg.at[mine, :], hg.at[mine, :])
    arrive(got)

    vs[0:432, :] = nt(s9c[...], glw[...])

    def rows64(b):
        return pl.ds(pl.multiple_of(b * 64, 64), 64)

    def rows256(b):
        return pl.ds(pl.multiple_of(b * 256, 256), 256)

    def grad_expand(i, carry):
        expand(glw, gx, i)
        return carry

    def input_step(i, carry):
        total = None
        for dx in range(3):
            field = gx[:, span(i, (2 - dx) * LAYER)]
            term = nn(wb_ref[dx * 144 : dx * 144 + 144, :], field)
            total = term if total is None else total + term
        conv = jnp.zeros((16, 512), F32)
        for j, (dy, dz) in enumerate(taps):
            shift = (dy * 16 + dz) % 512
            slab = total[j * 16 : j * 16 + 16]
            slab = pltpu.roll(slab, shift, 1) if shift else slab
            conv = conv + jnp.where(in_layer(512, -dy, -dz), slab, 0.0)
        own_grad = gx[mine, span(i, LAYER)].astype(F32)
        gf_ref[:, span(i)] = own_grad + jnp.where(ss_ref[:, span(i)] >= 0, conv, 0.0)
        return carry

    def pair_send(src, dst, n):
        return send(src, dst, red_s.at[n], red_r.at[n], {"vox_2": 1 - core})

    def x_send(src_of, dst, n):
        copies = []
        for r in (2, 1, 3):
            p = lax.rem(x + r, 4)
            copies.append(send(src_of(p), dst, red_s.at[n + r], red_r.at[n + r], to_x(p)))
        return copies

    got = [pair_send(vs.at[rows256(1 - core), :], half, 0)]
    arrive(got)
    pair[...] = (vs[rows256(core), :] + half[...]).astype(BF)
    quad[x] = pair[rows64(x), :]
    got = x_send(lambda p: pair.at[rows64(p), :], quad.at[x], 0)
    drain()
    lax.fori_loop(0, 8, grad_expand, 0)
    arrive(got)
    total = quad[0].astype(F32)
    for i in range(1, 4):
        total = total + quad[i].astype(F32)
    own64[...] = total.astype(BF)
    zsrc[z] = own64[...]
    got = exchange(14, z, to_z, lambda p: own64, zsrc.at[z])
    drain()
    arrive(got_halo)
    gx[:, 0:LAYER] = hg[:, 0:LAYER]
    gx[:, LAYER + CELLS : EXT] = hg[:, LAYER : 2 * LAYER]
    lax.fori_loop(0, 6, input_step, 0)
    arrive(got)
    total = zsrc[0].astype(F32)
    for i in range(1, 8):
        total = total + zsrc[i].astype(F32)
    zall[...] = total.astype(BF)
    back256[rows64(x), :] = zall[...]
    got = x_send(lambda p: zall, back256.at[rows64(x), :], 4)
    lax.fori_loop(6, 8, input_step, 0)
    drain()
    arrive(got)
    got = [pair_send(back256, back64, 8)]
    vv_ref[rows256(core), :] = back256[...].astype(F32)
    drain()
    arrive(got)
    vv_ref[rows256(1 - core), :] = back64[...].astype(F32)
    drain()
    drain()


def store_kernel(bo_ref, gf_ref, vv_ref, bo_out, gf_out, gc_out, gq_out, go_out, sem):
    stores = [
        pltpu.make_async_copy(src, dst, sem.at[i])
        for i, (src, dst) in enumerate(
            (
                (gf_ref, gf_out), (vv_ref.at[0:432, :], gc_out), (vv_ref.at[432:480, :], gq_out),
                (vv_ref.at[480:496, :], go_out), (bo_ref, bo_out),
            )
        )
    ]
    for store in stores:
        store.start()
    for store in stores:
        store.wait()


def body(
    features, conv_weight, qkv_weight, out_weight, cotangent, neighbours, send_slot, recv_slot
):
    wb = jnp.transpose(conv_weight, (0, 2, 1)).reshape(432, 128)
    w2 = jnp.transpose(qkv_weight, (0, 2, 1)).reshape(48, 128)

    def buf(*shape):
        return pltpu.VMEM(shape, BF)

    def wide(*shape):
        return pltpu.VMEM(shape, F32)

    scratch = [
        buf(16, CELLS), pltpu.VMEM((1, CELLS), jnp.int32), pltpu.VMEM((1, SLOTS), jnp.int32),
        buf(16, SLOTS), buf(432, 128), buf(48, 128), buf(16, 128),
        buf(SLOTS, CELLS), buf(SLOTS, SLOTS),
        buf(128, EXT), buf(128, 512), buf(2, 16, LAYER), buf(16, CELLS),
        buf(128, SLOTS), buf(128, 512), buf(8, 16, 512), buf(432, 128),
        buf(432, 20 * LAYER), buf(432, SLOTS), buf(16, CELLS), wide(16, SLOTS),
        buf(8, 16, 128), buf(8, 16, 128), buf(8, 16, 128), buf(8, 16, 128),
        buf(128, SLOTS), buf(128, SLOTS), buf(64, 128), buf(8, 64, 128),
        buf(SLOTS, 128), buf(128, SLOTS), buf(128, SLOTS), buf(48, SLOTS),
        buf(16, SLOTS), wide(SLOTS, 256), buf(SLOTS, 256), buf(SLOTS, 256),
        buf(64, SLOTS), wide(32, SLOTS), buf(128, SLOTS),
        buf(8, 32, 128), buf(8, 64, 128), buf(8, 32, 128),
        wide(16, SLOTS), buf(8, 16, 128), buf(8, 16, 128),
        buf(128, SLOTS), buf(128, EXT), buf(16, 512), buf(2, 16, LAYER), buf(128, 512),
        wide(512, 128), buf(8, 16, 128), wide(256, 128), buf(256, 128),
        buf(4, 64, 128), buf(64, 128), buf(8, 64, 128), buf(64, 128),
        buf(256, 128), buf(256, 128),
        buf(16, CELLS), buf(16, CELLS),
        pltpu.SemaphoreType.DMA((7,)),
        pltpu.SemaphoreType.DMA((16, 8)), pltpu.SemaphoreType.DMA((16, 8)),
        pltpu.SemaphoreType.DMA((4,)), pltpu.SemaphoreType.DMA((4,)),
        pltpu.SemaphoreType.DMA((9,)), pltpu.SemaphoreType.DMA((9,)),
    ]
    hbm = pl.BlockSpec(memory_space=pltpu.HBM)
    vmem = pl.BlockSpec(memory_space=pltpu.VMEM)
    block_out, grad_features, sums = pl.pallas_call(
        whole_kernel,
        out_shape=(
            jax.ShapeDtypeStruct((16, SLOTS), BF),
            jax.ShapeDtypeStruct((16, CELLS), F32),
            jax.ShapeDtypeStruct((512, 128), F32),
        ),
        in_specs=[hbm] * 7,
        out_specs=(vmem, vmem, vmem),
        scratch_shapes=scratch,
        compiler_params=pltpu.CompilerParams(
            collective_id=0, has_side_effects=True, vmem_limit_bytes=48 * 1024 * 1024
        ),
    )(
        *(
            pltpu.with_memory_space_constraint(array, pltpu.HBM)
            for array in (
                features, send_slot.reshape(1, CELLS), recv_slot.reshape(1, SLOTS), cotangent,
                wb, w2, out_weight,
            )
        )
    )
    block_out, grad_features, grad_conv, grad_qkv, grad_out = pl.pallas_call(
        store_kernel,
        out_shape=(
            jax.ShapeDtypeStruct((16, SLOTS), BF),
            jax.ShapeDtypeStruct((16, CELLS), F32),
            jax.ShapeDtypeStruct((432, 128), F32),
            jax.ShapeDtypeStruct((48, 128), F32),
            jax.ShapeDtypeStruct((16, 128), F32),
        ),
        in_specs=[vmem] * 3,
        out_specs=(hbm,) * 5,
        scratch_shapes=[pltpu.SemaphoreType.DMA((5,))],
        compiler_params=pltpu.CompilerParams(vmem_limit_bytes=4 * 1024 * 1024),
    )(block_out, grad_features, sums)
    grad_conv = jnp.transpose(grad_conv.reshape(27, 16, 128), (0, 2, 1))
    grad_qkv = jnp.transpose(grad_qkv.reshape(3, 16, 128), (0, 2, 1))
    return (block_out, grad_features, grad_conv, grad_qkv, grad_out)


def solution(mesh):
    torus = Mesh(mesh.devices.reshape(8, 4, 2, mesh.shape["ch"]), ("vox_0", "vox_1", "vox_2", "ch"))
    placed = (
        P("ch", VOX),
        P(None, None, "ch"),
        P(None, None, "ch"),
        P("ch", None),
        P("ch", VOX),
        P(None, VOX),
        P(VOX),
        P(VOX),
    )
    return jax.shard_map(
        body,
        mesh=torus,
        in_specs=placed,
        out_specs=(
            P("ch", VOX),
            P("ch", VOX),
            P(None, None, "ch"),
            P(None, None, "ch"),
            P("ch", None),
        ),
        check_vma=False,
    )
```

```python
import jax
import jax.numpy as jnp
from jax import lax
from jax.experimental import pallas as pl
from jax.experimental.pallas import tpu as pltpu
from jax.sharding import Mesh
from jax.sharding import PartitionSpec as P

MESH = pl.DeviceIdType.MESH
VOX = ("vox_0", "vox_1", "vox_2")
BF = jnp.bfloat16
F32 = jnp.float32
CELLS = 4096
LAYER = 256
EXT = CELLS + 2 * LAYER
SLOTS = 1024
ORDER = (4, 3, 5, 2, 6, 1, 7)


def nn(a, b):
    return jnp.dot(a, b, preferred_element_type=F32)


def nt(a, b):
    return lax.dot_general(a, b, (((1,), (1,)), ((), ())), preferred_element_type=F32)


def tn(a, b):
    return lax.dot_general(a, b, (((0,), (0,)), ((), ())), preferred_element_type=F32)


def lanes(shape):
    return lax.broadcasted_iota(jnp.int32, shape, 1)


def swap_blocks(tiles):
    flat = tiles.reshape(128, 128)
    turned = [flat if s == 0 else pltpu.roll(flat, s * 16, 1) for s in range(8)]
    block = lanes((16, 128)) // 16
    out = []
    for j in range(8):
        tile = turned[(0 - j) % 8][0:16]
        for i in range(1, 8):
            tile = jnp.where(block == i, turned[(i - j) % 8][i * 16 : i * 16 + 16], tile)
        out.append(tile)
    return out


def in_layer(width, dy, dz):
    cell = lanes((16, width))
    row = (cell // 16) % 16 + dy
    col = cell % 16 + dz
    return (row >= 0) & (row < 16) & (col >= 0) & (col < 16)


def whole_kernel(
    f_in, ss_in, rs_in, cot_in, wb_in, w2_in, ow_in,
    bo_ref, gf_ref, vv_ref,
    f_ref, ss_ref, rs_ref, cot_ref, wb_ref, w2_ref, ow_ref,
    onehot, pick, fx, hx, hl, fm, fc, wt, aw, w9, s27, s9c, layer, s1acc,
    s1, a1, t1, a2, gw, cw, mine2, ww,
    kvt, qq, gg, qkv, gaw, lg, pr, sc, pk, acc, big, xs, ys, u1, alive, v1, d1,
    glw, gx, hf, hl2, hg, vs, e0, half, pair, quad, own64, zsrc, zall, back64, back256,
    pattern, high,
    in_sem, ex_s, ex_r, halo_s, halo_r, red_s, red_r,
):
    z = lax.axis_index("vox_0")
    x = lax.axis_index("vox_1")
    core = lax.axis_index("vox_2")
    xc = x * 2 + core
    y = lax.axis_index("ch")
    d = z * 8 + xc

    def to_y(p):
        return {"ch": p}

    def to_z(p):
        return {"vox_0": p}

    def to_x(p):
        return {"vox_1": p}

    def to_xc(p):
        return {"vox_1": p // 2, "vox_2": lax.rem(p, 2)}

    def to_d(p):
        return {"vox_0": p // 8, "vox_1": lax.rem(p, 8) // 2, "vox_2": lax.rem(p, 2)}

    after, before = lax.rem(d + 1, 64), lax.rem(d + 63, 64)

    loads = [
        pltpu.make_async_copy(src, dst, in_sem.at[i])
        for i, (src, dst) in enumerate(
            (
                (ss_in, ss_ref), (f_in, f_ref), (wb_in, wb_ref), (rs_in, rs_ref),
                (cot_in, cot_ref), (w2_in, w2_ref), (ow_in, ow_ref),
            )
        )
    ]
    for load in loads:
        load.start()

    barrier = pltpu.get_barrier_semaphore()
    for r in range(1, 8):
        for me, where in ((y, to_y), (z, to_z), (xc, to_xc)):
            pl.semaphore_signal(
                barrier, inc=1, device_id=where(lax.rem(me + r, 8)), device_id_type=MESH
            )
    for p in (after, before):
        pl.semaphore_signal(barrier, inc=1, device_id=to_d(p), device_id_type=MESH)

    fresh, old = [], []

    def send(src, dst, s_sem, r_sem, where):
        copy = pltpu.make_async_remote_copy(
            src_ref=src, dst_ref=dst, send_sem=s_sem, recv_sem=r_sem,
            device_id=where, device_id_type=MESH,
        )
        copy.start()
        fresh.append(copy)
        return copy

    def drain():
        for copy in old:
            copy.wait_send()
        old[:] = fresh
        fresh.clear()

    def exchange(phase, me, where, src_of, dst):
        copies = []
        for r in ORDER:
            p = lax.rem(me + r, 8)
            copies.append(
                send(src_of(p), dst, ex_s.at[phase, r], ex_r.at[phase, r], where(p))
            )
        return copies

    def arrive(copies):
        for copy in copies:
            copy.wait_recv()

    def rows16(b):
        return pl.ds(pl.multiple_of(b * 16, 16), 16)

    def tile(b):
        return pl.ds(pl.multiple_of(b * 128, 128), 128)

    def span(i, start=0, size=512):
        return pl.ds(pl.multiple_of(i * 512 + start, 256), size)

    mine = rows16(y)
    loads[0].wait()

    low = lax.broadcasted_iota(jnp.int32, (16, CELLS), 0)
    pattern[...] = jnp.where(low == (ss_ref[...] & 15), 1.0, 0.0).astype(BF)
    high[...] = jnp.broadcast_to((ss_ref[...] >> 4).astype(F32), (16, CELLS)).astype(BF)

    def onehot_step(i, carry):
        at = pl.multiple_of(i * 16, 16)
        here = high[...] == i.astype(F32).astype(BF)
        onehot[pl.ds(at, 16), :] = jnp.where(here, pattern[...], jnp.zeros((), BF))
        return carry

    lax.fori_loop(0, 64, onehot_step, 0)

    loads[1].wait()
    fm[...] = jnp.where(ss_ref[...] >= 0, f_ref[...].astype(F32), 0.0).astype(BF)

    loads[2].wait()
    weights = jnp.concatenate([wb_ref[...].astype(F32), jnp.zeros((80, 128), F32)], axis=0)
    for t in range(4):
        wt[:, t * 128 : t * 128 + 128] = weights[t * 128 : t * 128 + 128, :].T.astype(BF)

    pl.semaphore_wait(barrier, 23)
    halo = [
        send(fm.at[:, CELLS - LAYER : CELLS], hl.at[0], halo_s.at[0], halo_r.at[0], to_d(after)),
        send(fm.at[:, 0:LAYER], hl.at[1], halo_s.at[1], halo_r.at[1], to_d(before)),
    ]
    got_aw = exchange(11, y, to_y, lambda p: wt.at[rows16(p), :], aw.at[y])
    def compact_step(i, carry):
        at = pl.multiple_of(i * 256, 256)
        fc[mine, pl.ds(at, 256)] = nt(fm[...], onehot[pl.ds(at, 256), :]).astype(BF)
        return carry


    lax.fori_loop(0, 4, compact_step, 0)
    got = exchange(0, y, to_y, lambda p: fc.at[mine, :], fc.at[mine, :])

    aw[y] = wt[mine, :]
    for load in loads[3:]:
        load.wait()
    live = rs_ref[...] >= 0
    mine2[0:48, :] = w2_ref[...]
    mine2[48:64, :] = ow_ref[...]
    ww[y] = mine2[...]
    source = rs_ref[...]
    route = (source >> 4) & 7
    spot = jnp.where(live, route * 128 + ((source >> 7) & 7) * 16 + (source & 15), -1)

    arrive(halo)
    hx[mine, 0:LAYER] = jnp.where(d == 0, 0.0, hl[0].astype(F32)).astype(BF)
    hx[mine, LAYER : 2 * LAYER] = jnp.where(d == 63, 0.0, hl[1].astype(F32)).astype(BF)
    got_hx = exchange(12, y, to_y, lambda p: hx.at[mine, :], hx.at[mine, :])

    taps = [(dy, dz) for dy in (-1, 0, 1) for dz in (-1, 0, 1)]

    def shifted(values, width, put):
        for j, (dy, dz) in enumerate(taps):
            shift = -(dy * 16 + dz) % width
            slab = pltpu.roll(values, shift, 1) if shift else values
            slab = jnp.where(in_layer(width, dy, dz), slab, 0.0).astype(BF)
            for dx in range(3):
                put(dx, dx * 144 + j * 16, slab)

    def shifted_step(i, carry):
        def put(dx, row, slab):
            s27[row : row + 16, span(i, (3 - dx) * LAYER)] = slab

        shifted(fm[:, span(i)].astype(F32), 512, put)
        return carry

    lax.fori_loop(0, 8, shifted_step, 0)
    edges = hx[mine, :].astype(F32)

    def put_left(dx, row, slab):
        s27[row : row + 16, (2 - dx) * LAYER : (3 - dx) * LAYER] = slab[:, 0:LAYER]

    def put_right(dx, row, slab):
        s27[row : row + 16, (19 - dx) * LAYER : (20 - dx) * LAYER] = slab[:, LAYER : 2 * LAYER]

    shifted(edges, 512, put_left)
    shifted(edges, 512, put_right)

    def s9c_step(i, carry):
        at = pl.multiple_of(i * 256, 256)
        s9c[:, pl.ds(at, 256)] = nt(
            s27[:, 512 : 512 + CELLS], onehot[pl.ds(at, 256), :]
        ).astype(BF)
        return carry

    def pick_step(i, carry):
        at = pl.multiple_of(i * 16, 16)
        ids = lax.broadcasted_iota(jnp.int32, (16, SLOTS), 0) + at
        pick[pl.ds(at, 16), :] = jnp.where(ids == spot, 1.0, 0.0).astype(BF)
        return carry

    lax.fori_loop(0, 64, pick_step, 0)
    masked = jnp.where(live, cot_ref[...].astype(F32), 0.0).astype(BF)
    first = lax.broadcasted_iota(jnp.int32, (16, SLOTS), 0) == 0
    moved = jnp.concatenate([masked, jnp.where(first, 1.0, 0.0).astype(BF)], axis=0)
    moved = nt(moved, pick[...])
    cw[mine, :] = moved[0:16].astype(BF)
    alive[...] = moved[16:32]
    qq[...] = jnp.zeros((128, SLOTS), BF)
    gg[...] = jnp.zeros((128, SLOTS), BF)
    s1acc[...] = jnp.zeros((16, SLOTS), F32)
    acc[...] = jnp.zeros((32, SLOTS), F32)

    arrive(got_aw)
    for t in range(4):
        for k, part in enumerate(swap_blocks(aw[:, :, t * 128 : t * 128 + 128].astype(F32))):
            if t * 8 + k < 27:
                at = (t * 8 + k) * 16
                w9[at : at + 16, :] = part.astype(BF)

    arrive(got)
    got_ww = exchange(1, y, to_y, lambda p: mine2, ww.at[y])
    got_cw = exchange(2, y, to_y, lambda p: cw.at[mine, :], cw.at[mine, :])
    drain()

    def expand(src, dst, i):
        dst[:, span(i, LAYER)] = nn(src[...], onehot[:, span(i)]).astype(BF)

    def conv(i):
        total = None
        for dx in range(3):
            field = fx[:, span(i, dx * LAYER)]
            term = nn(w9[dx * 144 : dx * 144 + 144, :], field)
            total = term if total is None else total + term
        out = fm[:, span(i)].astype(F32)
        summed = jnp.zeros((16, 512), F32)
        for j, (dy, dz) in enumerate(taps):
            shift = -(dy * 16 + dz) % 512
            slab = total[j * 16 : j * 16 + 16]
            slab = pltpu.roll(slab, shift, 1) if shift else slab
            summed = summed + jnp.where(in_layer(512, dy, dz), slab, 0.0)
        layer[:, span(i)] = (out + summed).astype(BF)

    def pack(i):
        s1acc[...] += nt(layer[:, span(i)], onehot[:, span(i)])

    for i in range(4):
        expand(fc, fx, i)
    conv(1)

    def conv_step(i, carry):
        pack(i - 1)
        conv(i)
        expand(fc, fx, i + 2)
        return carry

    lax.fori_loop(2, 6, conv_step, 0)
    pack(5)
    conv(6)
    pack(6)
    arrive(got_hx)
    fx[:, 0:LAYER] = hx[:, 0:LAYER]
    fx[:, LAYER + CELLS : EXT] = hx[:, LAYER : 2 * LAYER]
    conv(0)
    pack(0)
    conv(7)
    pack(7)
    packed = s1acc[...].astype(BF)
    for t in range(8):
        s1[t] = packed[:, t * 128 : t * 128 + 128]
    a1[z] = s1[z]
    got = exchange(3, z, to_z, lambda p: s1.at[p], a1.at[z])
    lax.fori_loop(0, 2, s9c_step, 0)

    drain()
    arrive(got)
    for j, part in enumerate(swap_blocks(a1[...].astype(F32))):
        t1[j] = part.astype(BF)
    a2[xc] = t1[xc]
    got = exchange(4, xc, to_xc, lambda p: t1.at[p], a2.at[xc])
    drain()
    arrive(got)
    arrived = jnp.concatenate([a2[i] for i in range(8)], axis=1)
    gw[mine, :] = arrived
    got = exchange(5, y, to_y, lambda p: gw.at[mine, :], gw.at[mine, :])
    drain()
    arrive(got_cw)
    arrive(got_ww)
    ga = nn(ow_ref[...], cw[...]).astype(BF)
    gaw[...] = ga
    gg[32:48, :] = (ga.astype(F32) * 0.25).astype(BF)
    lax.fori_loop(2, 4, s9c_step, 0)
    arrive(got)

    whole = gw[...].astype(F32)
    mean = jnp.mean(whole, axis=0, keepdims=True)
    centred = whole - mean
    var = jnp.mean(centred * centred, axis=0, keepdims=True)
    normed = (centred * lax.rsqrt(var + 1e-05)).astype(BF)
    big[...] = normed
    rows = nn(w2_ref[...], normed).astype(BF)
    qkv[...] = rows
    qq[0:16, :] = (rows[0:16].astype(F32) * 0.25).astype(BF)
    row = lax.broadcasted_iota(jnp.int32, (16, SLOTS), 0)
    qq[16:32, :] = jnp.where(row == 0, 1.0, 0.0).astype(BF)
    bias = jnp.where((row == 0) & (alive[...] < 0.5), -1e30, 0.0)
    stacked = jnp.concatenate(
        [
            rows[16:32].astype(F32),
            bias,
            rows[32:48].astype(F32),
            jnp.zeros((80, SLOTS), F32),
        ],
        axis=0,
    )
    for t in range(8):
        kvt[t * 128 : t * 128 + 128, :] = stacked[:, t * 128 : t * 128 + 128].T.astype(BF)

    def attend_step(i, carry):
        at = pl.ds(pl.multiple_of(i * 256, 256), 256)
        top = None
        for c in range(4):
            cells = slice(c * 256, c * 256 + 256)
            logits = nn(kvt[cells, :], qq[:, at])
            lg[cells, :] = logits
            most = jnp.max(logits.reshape(32, 8, 256), axis=0)
            top = most if top is None else jnp.maximum(top, most)
        top = jnp.max(top, axis=0, keepdims=True)
        total = jnp.zeros((8, 256), F32)
        for c in range(16):
            cells = slice(c * 64, c * 64 + 64)
            exponents = jnp.exp(lg[cells, :] - top)
            lg[cells, :] = exponents
            total = total + jnp.sum(exponents.reshape(8, 8, 256), axis=0)
        inverse_total = 1.0 / jnp.sum(total, axis=0, keepdims=True)
        for c in range(16):
            cells = slice(c * 64, c * 64 + 64)
            pr[cells, :] = (lg[cells, :] * inverse_total).astype(BF)
        attended = nn(qkv[32:48, :], pr[...])
        pk[0:16, at] = attended.astype(BF)
        inner = jnp.sum(attended * gg[32:48, at].astype(F32), axis=0, keepdims=True)
        acc[16:32, :] += nt(gaw[:, at], pr[...])
        for c in range(4):
            cells = slice(c * 256, c * 256 + 256)
            grad_logits = nn(kvt[cells, :], gg[:, at])
            sc[cells, :] = (pr[cells, :].astype(F32) * (grad_logits - inner)).astype(BF)
        pk[16:32, at] = nn(qkv[16:32, :], sc[...]).astype(BF)
        acc[0:16, :] += nt(qkv[0:16, at], sc[...])
        return carry

    lax.fori_loop(0, 4, attend_step, 0)
    pk[32:64, :] = acc[...].astype(BF)

    ys[y] = pk[:, tile(y)]
    got = exchange(6, y, to_y, lambda p: pk.at[:, tile(p)], ys.at[y])
    drain()
    vs[432:480, :] = nt(pk[16:64, :], big[...])
    vs[480:496, :] = nt(pk[0:16, :], cw[...])
    vs[496:512, :] = jnp.zeros((16, 128), F32)
    own_slots = tile(y)
    part = gw[:, own_slots].astype(F32)
    mean = jnp.mean(part, axis=0, keepdims=True)
    centred = part - mean
    var = jnp.mean(centred * centred, axis=0, keepdims=True)
    inverse = lax.rsqrt(var + 1e-05)
    normal = centred * inverse
    cot = cw[:, own_slots].astype(F32)
    live_part = alive[0:1, own_slots] > 0.5
    arrive(got)
    mixed = tn(ww[:, 48:64, :].reshape(128, 128), ys[:, 0:16, :].reshape(128, 128))
    grad = None
    for i in range(3):
        term = tn(
            ww[:, i * 16 : i * 16 + 16, :].reshape(128, 128),
            ys[:, 16 + i * 16 : 32 + i * 16, :].reshape(128, 128),
        )
        grad = term if grad is None else grad + term
    grad = grad.astype(BF).astype(F32)
    grad_ln = inverse * (
        grad
        - jnp.mean(grad, axis=0, keepdims=True)
        - normal * jnp.mean(grad * normal, axis=0, keepdims=True)
    )
    back = jnp.where(live_part, cot + grad_ln, 0.0).astype(BF)
    block = jnp.where(live_part, part + mixed, 0.0).astype(BF)
    xs[:, 0:16, :] = back.reshape(8, 16, 128)
    xs[:, 16:32, :] = block.reshape(8, 16, 128)
    u1[y] = xs[y]
    got = exchange(7, y, to_y, lambda p: xs.at[p], u1.at[y])
    drain()
    arrive(got)
    v1[xc] = u1[xc, 0:16, :]
    got = exchange(8, xc, to_xc, lambda p: u1.at[p, 0:16, :], v1.at[xc])
    drain()
    bo_ref[...] = nn(jnp.concatenate([u1[i, 16:32] for i in range(8)], axis=1), pick[...]).astype(BF)
    arrive(got)
    for j, piece in enumerate(swap_blocks(v1[...].astype(F32))):
        d1[j] = piece.astype(BF)
    e0[z] = d1[z]
    got = exchange(9, z, to_z, lambda p: d1.at[p], e0.at[z])
    drain()
    arrive(got)
    slots = jnp.concatenate([e0[i] for i in range(8)], axis=1)
    glw[mine, :] = slots
    got = exchange(10, y, to_y, lambda p: glw.at[mine, :], glw.at[mine, :])
    drain()
    hf[:, 0:LAYER] = nn(slots, onehot[:, 0:LAYER]).astype(BF)
    hf[:, LAYER : 2 * LAYER] = nn(slots, onehot[:, CELLS - LAYER : CELLS]).astype(BF)
    halo = [
        send(hf.at[:, LAYER : 2 * LAYER], hl2.at[0], halo_s.at[2], halo_r.at[2], to_d(after)),
        send(hf.at[:, 0:LAYER], hl2.at[1], halo_s.at[3], halo_r.at[3], to_d(before)),
    ]
    arrive(halo)
    hg[mine, 0:LAYER] = jnp.where(d == 0, 0.0, hl2[0].astype(F32)).astype(BF)
    hg[mine, LAYER : 2 * LAYER] = jnp.where(d == 63, 0.0, hl2[1].astype(F32)).astype(BF)
    got_halo = exchange(13, y, to_y, lambda p: hg.at[mine, :], hg.at[mine, :])
    arrive(got)

    vs[0:432, :] = nt(s9c[...], glw[...])

    def rows64(b):
        return pl.ds(pl.multiple_of(b * 64, 64), 64)

    def rows256(b):
        return pl.ds(pl.multiple_of(b * 256, 256), 256)

    def grad_expand(i, carry):
        expand(glw, gx, i)
        return carry

    def input_step(i, carry):
        total = None
        for dx in range(3):
            field = gx[:, span(i, (2 - dx) * LAYER)]
            term = nn(wb_ref[dx * 144 : dx * 144 + 144, :], field)
            total = term if total is None else total + term
        conv = jnp.zeros((16, 512), F32)
        for j, (dy, dz) in enumerate(taps):
            shift = (dy * 16 + dz) % 512
            slab = total[j * 16 : j * 16 + 16]
            slab = pltpu.roll(slab, shift, 1) if shift else slab
            conv = conv + jnp.where(in_layer(512, -dy, -dz), slab, 0.0)
        own_grad = gx[mine, span(i, LAYER)].astype(F32)
        gf_ref[:, span(i)] = own_grad + jnp.where(ss_ref[:, span(i)] >= 0, conv, 0.0)
        return carry

    def pair_send(src, dst, n):
        return send(src, dst, red_s.at[n], red_r.at[n], {"vox_2": 1 - core})

    def x_send(src_of, dst, n):
        copies = []
        for r in (2, 1, 3):
            p = lax.rem(x + r, 4)
            copies.append(send(src_of(p), dst, red_s.at[n + r], red_r.at[n + r], to_x(p)))
        return copies

    got = [pair_send(vs.at[rows256(1 - core), :], half, 0)]
    arrive(got)
    pair[...] = (vs[rows256(core), :] + half[...]).astype(BF)
    quad[x] = pair[rows64(x), :]
    got = x_send(lambda p: pair.at[rows64(p), :], quad.at[x], 0)
    drain()
    lax.fori_loop(0, 8, grad_expand, 0)
    arrive(got)
    total = quad[0].astype(F32)
    for i in range(1, 4):
        total = total + quad[i].astype(F32)
    own64[...] = total.astype(BF)
    zsrc[z] = own64[...]
    got = exchange(14, z, to_z, lambda p: own64, zsrc.at[z])
    drain()
    arrive(got_halo)
    gx[:, 0:LAYER] = hg[:, 0:LAYER]
    gx[:, LAYER + CELLS : EXT] = hg[:, LAYER : 2 * LAYER]
    lax.fori_loop(0, 6, input_step, 0)
    arrive(got)
    total = zsrc[0].astype(F32)
    for i in range(1, 8):
        total = total + zsrc[i].astype(F32)
    zall[...] = total.astype(BF)
    back256[rows64(x), :] = zall[...]
    got = x_send(lambda p: zall, back256.at[rows64(x), :], 4)
    lax.fori_loop(6, 8, input_step, 0)
    drain()
    arrive(got)
    got = [pair_send(back256, back64, 8)]
    vv_ref[rows256(core), :] = back256[...].astype(F32)
    drain()
    arrive(got)
    vv_ref[rows256(1 - core), :] = back64[...].astype(F32)
    drain()
    drain()


def store_kernel(bo_ref, gf_ref, vv_ref, bo_out, gf_out, gc_out, gq_out, go_out, sem):
    stores = [
        pltpu.make_async_copy(src, dst, sem.at[i])
        for i, (src, dst) in enumerate(
            (
                (gf_ref, gf_out), (vv_ref.at[0:432, :], gc_out), (vv_ref.at[432:480, :], gq_out),
                (vv_ref.at[480:496, :], go_out), (bo_ref, bo_out),
            )
        )
    ]
    for store in stores:
        store.start()
    for store in stores:
        store.wait()


def body(
    features, conv_weight, qkv_weight, out_weight, cotangent, neighbours, send_slot, recv_slot
):
    wb = jnp.transpose(conv_weight, (0, 2, 1)).reshape(432, 128)
    w2 = jnp.transpose(qkv_weight, (0, 2, 1)).reshape(48, 128)

    def buf(*shape):
        return pltpu.VMEM(shape, BF)

    def wide(*shape):
        return pltpu.VMEM(shape, F32)

    scratch = [
        buf(16, CELLS), pltpu.VMEM((1, CELLS), jnp.int32), pltpu.VMEM((1, SLOTS), jnp.int32),
        buf(16, SLOTS), buf(432, 128), buf(48, 128), buf(16, 128),
        buf(SLOTS, CELLS), buf(SLOTS, SLOTS),
        buf(128, EXT), buf(128, 512), buf(2, 16, LAYER), buf(16, CELLS),
        buf(128, SLOTS), buf(128, 512), buf(8, 16, 512), buf(432, 128),
        buf(432, 20 * LAYER), buf(432, SLOTS), buf(16, CELLS), wide(16, SLOTS),
        buf(8, 16, 128), buf(8, 16, 128), buf(8, 16, 128), buf(8, 16, 128),
        buf(128, SLOTS), buf(128, SLOTS), buf(64, 128), buf(8, 64, 128),
        buf(SLOTS, 128), buf(128, SLOTS), buf(128, SLOTS), buf(48, SLOTS),
        buf(16, SLOTS), wide(SLOTS, 256), buf(SLOTS, 256), buf(SLOTS, 256),
        buf(64, SLOTS), wide(32, SLOTS), buf(128, SLOTS),
        buf(8, 32, 128), buf(8, 64, 128), buf(8, 32, 128),
        wide(16, SLOTS), buf(8, 16, 128), buf(8, 16, 128),
        buf(128, SLOTS), buf(128, EXT), buf(16, 512), buf(2, 16, LAYER), buf(128, 512),
        wide(512, 128), buf(8, 16, 128), wide(256, 128), buf(256, 128),
        buf(4, 64, 128), buf(64, 128), buf(8, 64, 128), buf(64, 128),
        buf(256, 128), buf(256, 128),
        buf(16, CELLS), buf(16, CELLS),
        pltpu.SemaphoreType.DMA((7,)),
        pltpu.SemaphoreType.DMA((16, 8)), pltpu.SemaphoreType.DMA((16, 8)),
        pltpu.SemaphoreType.DMA((4,)), pltpu.SemaphoreType.DMA((4,)),
        pltpu.SemaphoreType.DMA((9,)), pltpu.SemaphoreType.DMA((9,)),
    ]
    hbm = pl.BlockSpec(memory_space=pltpu.HBM)
    vmem = pl.BlockSpec(memory_space=pltpu.VMEM)
    block_out, grad_features, sums = pl.pallas_call(
        whole_kernel,
        out_shape=(
            jax.ShapeDtypeStruct((16, SLOTS), BF),
            jax.ShapeDtypeStruct((16, CELLS), F32),
            jax.ShapeDtypeStruct((512, 128), F32),
        ),
        in_specs=[hbm] * 7,
        out_specs=(vmem, vmem, vmem),
        scratch_shapes=scratch,
        compiler_params=pltpu.CompilerParams(
            collective_id=0, has_side_effects=True, vmem_limit_bytes=48 * 1024 * 1024
        ),
    )(
        *(
            pltpu.with_memory_space_constraint(array, pltpu.HBM)
            for array in (
                features, send_slot.reshape(1, CELLS), recv_slot.reshape(1, SLOTS), cotangent,
                wb, w2, out_weight,
            )
        )
    )
    block_out, grad_features, grad_conv, grad_qkv, grad_out = pl.pallas_call(
        store_kernel,
        out_shape=(
            jax.ShapeDtypeStruct((16, SLOTS), BF),
            jax.ShapeDtypeStruct((16, CELLS), F32),
            jax.ShapeDtypeStruct((432, 128), F32),
            jax.ShapeDtypeStruct((48, 128), F32),
            jax.ShapeDtypeStruct((16, 128), F32),
        ),
        in_specs=[vmem] * 3,
        out_specs=(hbm,) * 5,
        scratch_shapes=[pltpu.SemaphoreType.DMA((5,))],
        compiler_params=pltpu.CompilerParams(vmem_limit_bytes=4 * 1024 * 1024),
    )(block_out, grad_features, sums)
    grad_conv = jnp.transpose(grad_conv.reshape(27, 16, 128), (0, 2, 1))
    grad_qkv = jnp.transpose(grad_qkv.reshape(3, 16, 128), (0, 2, 1))
    return (block_out, grad_features, grad_conv, grad_qkv, grad_out)


def solution(mesh):
    torus = Mesh(mesh.devices.reshape(8, 4, 2, mesh.shape["ch"]), ("vox_0", "vox_1", "vox_2", "ch"))
    placed = (
        P("ch", VOX),
        P(None, None, "ch"),
        P(None, None, "ch"),
        P("ch", None),
        P("ch", VOX),
        P(None, VOX),
        P(VOX),
        P(VOX),
    )
    return jax.shard_map(
        body,
        mesh=torus,
        in_specs=placed,
        out_specs=(
            P("ch", VOX),
            P("ch", VOX),
            P(None, None, "ch"),
            P(None, None, "ch"),
            P("ch", None),
        ),
        check_vma=False,
    )
```
